128 devices in a mesh: rows: 64 (over y, x, z), feat: 2 (over core).
Axes of the slice: x: 4, y: 4, z: 4, core: 2. Of those that a mesh axis runs over, the one named last changes fastest.
Arguments:
- blocks: bfloat16 [8192, 8, 128, 128], P('rows', 'feat'), may hold values from -0.1875 to 0.1875
- col_index: int32 [8192, 8], P('rows', 'feat'), may hold values from 0 to 8191, as said below
- row_counts: int32 [8192, 2], P('rows', 'feat'), may hold values from 1 to 4, as said below
- labels: int32 [8192, 128], P('rows'), may hold values 0 or 1
- row_weight: float32 [8192, 128], P('rows'), may hold values from 0.3 to 9
- feature_scale: float32 [8192, 128], P('feat'), may hold values from 0.3 to 3
Outputs:
- solution: float32 [8192, 128], P('feat')
- last_resid: float32 [8192, 128], P('rows')
The draws below stay inside these ranges and needn't reach their ends.
Inputs may be any that keep to these rules, and one draw needn't show every extreme that they name: `col_index`: a block in slot j of a row block names a feature block of half j // 4, that is from (j // 4) * 4096 to (j // 4 + 1) * 4096 - 1. `row_counts`: some row block of every index of rows has 4 stored blocks in each half; slots from the count on are ignored.
All inputs are finite; a program needn't handle non-finite values. No bound on the sum of `labels` on one device may be relied on, other than what follows from the above.
Results may differ from the reference program's by a relative error of at most 0.0063.
Values may be sent and summed in bfloat16 or wider, within the bound.
No kernel may reach another device: no remote copies, remote signals or barrier semaphores. Data moves between devices by JAX's collectives and lax.ppermute only.
A program may use at most 64 MiB of HBM per device.

```python
import math
import jax
import jax.numpy as jnp
from jax import lax

RB_DEV = 128
BS = 128
KB = 4
ITERS = 2
NRB = 8192
NFB = 8192
FB_HALF = 4096
SLOTS = 8
N_ROWS = 64
N_FEAT = 2


def draw_col_index(key, part):
    first_key, second_key = jax.random.split(jax.random.fold_in(key, 11))
    halves = jnp.arange(SLOTS, dtype=jnp.int32) // KB
    picks = jax.random.randint(first_key, (NRB, SLOTS), 0, FB_HALF) + halves[None, :] * FB_HALF
    chosen = jax.random.randint(second_key, (), 0, NRB)
    row_ids = jnp.arange(NRB, dtype=jnp.int32)[:, None]
    slot_ids = jnp.arange(SLOTS, dtype=jnp.int32)[None, :]
    picks = jnp.where((row_ids == chosen) & (slot_ids == SLOTS - 1), NFB - 1, picks)
    picks = jnp.where((row_ids == chosen) & (slot_ids == 0), 0, picks)
    return picks.astype(jnp.int32)


def draw_row_counts(key, part):
    first_key, second_key = jax.random.split(jax.random.fold_in(key, 23))
    counts = jax.random.randint(first_key, (NRB, N_FEAT), 1, KB + 1)
    owners_total = NRB // RB_DEV
    chosen = jax.random.randint(second_key, (owners_total,), 0, RB_DEV)
    row_ids = jnp.arange(NRB, dtype=jnp.int32)
    full_row = row_ids % RB_DEV == chosen[row_ids // RB_DEV]
    counts = jnp.where(full_row[:, None], KB, counts)
    return counts.astype(jnp.int32)


def draw_row_weight(key, part):
    first_key = jax.random.fold_in(key, 37)
    position = jnp.arange(NRB, dtype=jnp.float32)[:, None] / NRB
    trend = jnp.exp(math.log(3.0) * position)
    base = jnp.exp(jax.random.uniform(first_key, (NRB, BS), jnp.float32, math.log(0.3), math.log(3.0)))
    return (base * trend).astype(jnp.float32)


def set_ends(entries, rng, smallest, largest):
    place = [jax.random.randint(jax.random.fold_in(rng, axis), (), 0, length) for axis, length in enumerate(entries.shape)]
    widest = entries.shape.index(max(entries.shape))
    neighbour = place[:widest] + [(place[widest] + 1) % entries.shape[widest]] + place[widest + 1:]
    return entries.at[tuple(place)].set(smallest).at[tuple(neighbour)].set(largest)


def level_of(stream_key, extent, cuts, least, top_value):
    loudness = 1.0
    for axis_at, shards_of in cuts:
        steps = jax.random.uniform(jax.random.fold_in(jax.random.fold_in(stream_key, 6), axis_at), (shards_of,), jnp.float32, least / len(cuts), top_value / len(cuts))
        loudness = loudness * jnp.repeat(jnp.exp(steps), extent[axis_at] // shards_of).reshape((-1,) + (1,) * (len(extent) - 1 - axis_at))
    return loudness


def gaussian(rng, dims, scale, bound, pieces=(), kind=jnp.bfloat16):
    entries = scale * jax.random.normal(rng, dims, jnp.float32)
    if pieces:
        entries = entries * level_of(rng, dims, pieces, -0.22, 0.18)
    return jnp.clip(entries, -bound, bound).astype(kind)


def setup_inputs(seed: int = 0) -> dict:
    keys = jax.random.split(jax.random.key(seed), 7)
    return {
        "blocks": gaussian(keys[0], (NRB, SLOTS, BS, BS), (BS * SLOTS) ** -0.5, 0.1875, ((0, 64), (1, 2))),
        "col_index": draw_col_index(jax.random.fold_in(keys[6], 71), 0),
        "row_counts": draw_row_counts(jax.random.fold_in(keys[6], 71), 0),
        "labels": set_ends((jax.random.randint(keys[3], (NRB, BS), 0, 2) < 1).astype(jnp.int32), jax.random.fold_in(keys[3], 1), 0, 1),
        "row_weight": draw_row_weight(jax.random.fold_in(keys[6], 71), 0),
        "feature_scale": jnp.clip(jnp.exp(math.log(3.0) - 2.3025851 * jax.random.uniform(keys[5], (NFB, BS), jnp.float32) ** level_of(keys[5], (NFB, BS), ((0, 2),), -0.2, 0.2)), 0.3, 3.0),
    }


def live_mask(col_index, row_counts):
    slot_ids = lax.broadcasted_iota(jnp.int32, col_index.shape, 1)
    counts = jnp.repeat(row_counts, KB, axis=1)
    return (slot_ids % KB < counts).astype(jnp.float32)

def apply_forward(blocks, col_index, live, scaled):

    def one_group(items):
        group_blocks, group_cols, group_live = items
        picked = scaled[group_cols].astype(jnp.float32)
        terms = jnp.einsum('rsij,rsj->rsi', group_blocks.astype(jnp.float32), picked)
        return lax.optimization_barrier(jnp.sum(terms * group_live[:, :, None], axis=1))
    parts = lax.map(one_group, (blocks.reshape(N_ROWS, RB_DEV, SLOTS, BS, BS), col_index.reshape(N_ROWS, RB_DEV, SLOTS), live.reshape(N_ROWS, RB_DEV, SLOTS)))
    return parts.reshape(NRB, BS)

def apply_transpose(blocks, col_index, live, rowed):

    def one_group(total, items):
        group_blocks, group_cols, group_live, group_rows = items
        terms = jnp.einsum('rsij,ri->rsj', group_blocks.astype(jnp.float32), group_rows.astype(jnp.float32))
        terms = terms * group_live[:, :, None]
        total = total + jax.ops.segment_sum(terms.reshape(-1, BS), group_cols.reshape(-1), num_segments=NFB)
        return (total, None)
    start = jnp.zeros((NFB, BS), jnp.float32)
    total, _ = lax.scan(one_group, start, (blocks.reshape(N_ROWS, RB_DEV, SLOTS, BS, BS), col_index.reshape(N_ROWS, RB_DEV, SLOTS), live.reshape(N_ROWS, RB_DEV, SLOTS), rowed.reshape(N_ROWS, RB_DEV, BS)))
    return total

def reference(blocks, col_index, row_counts, labels, row_weight, feature_scale):
    live = live_mask(col_index, row_counts)
    resid = row_weight * (2 * labels - 1).astype(jnp.float32)
    beta_now = jnp.sqrt(jnp.sum(resid * resid) + 1e-06)
    unit_rows = resid / beta_now
    rowed = (row_weight * resid).astype(jnp.bfloat16)
    total = apply_transpose(blocks, col_index, live, rowed)
    step_vec = feature_scale * total / beta_now
    alpha_now = jnp.sqrt(jnp.sum(step_vec * step_vec) + 1e-06)
    unit_feat = step_vec / alpha_now
    phi_bar = beta_now
    rho_bar = alpha_now
    search = unit_feat
    solution = jnp.zeros_like(unit_feat)
    for turn in range(ITERS):
        scaled = (feature_scale * unit_feat).astype(jnp.bfloat16)
        resid = row_weight * apply_forward(blocks, col_index, live, scaled) - alpha_now * unit_rows
        beta_now = jnp.sqrt(jnp.sum(resid * resid) + 1e-06)
        unit_rows = resid / beta_now
        rowed = (row_weight * resid).astype(jnp.bfloat16)
        total = apply_transpose(blocks, col_index, live, rowed)
        step_vec = feature_scale * total / beta_now - beta_now * unit_feat
        alpha_now = jnp.sqrt(jnp.sum(step_vec * step_vec) + 1e-06)
        unit_feat = step_vec / alpha_now
        rho_now = jnp.sqrt(rho_bar * rho_bar + beta_now * beta_now)
        cosine = rho_bar / rho_now
        sine_part = beta_now / rho_now
        theta_now = sine_part * alpha_now
        rho_bar = -cosine * alpha_now
        phi_now = cosine * phi_bar
        phi_bar = sine_part * phi_bar
        solution = solution + phi_now / rho_now * search
        search = unit_feat - theta_now / rho_now * search
    return (solution, resid)
```

```python
import functools

import jax
import jax.numpy as jnp
from jax import lax
from jax.experimental import pallas as pl
from jax.experimental.pallas import tpu as pltpu
from jax.sharding import PartitionSpec as P

F32 = jnp.float32
BF16 = jnp.bfloat16
EPS = 1e-06
META = 8
CHUNK = 16


def spread(value):
    full = jnp.broadcast_to(value, (META, 128))
    high = full.astype(BF16).astype(F32)
    rest = full - high
    mid = rest.astype(BF16).astype(F32)
    low = (rest - mid).astype(BF16).astype(F32)
    row = lax.broadcasted_iota(jnp.int32, (META, 128), 0)
    tile = jnp.where(row == 0, high, jnp.where(row == 1, mid, jnp.where(row == 2, low, 0.0)))
    return tile.astype(BF16)


def total_sum(x):
    return jnp.sum(jnp.sum(x, axis=0, keepdims=True), axis=1, keepdims=True)


def gathered_sum(tile):
    return jnp.sum(tile, axis=0, keepdims=True)[:, 0:1]


def backward_steps(own, blk, col, cnt, grow, tots, out, square):
    step = pl.program_id(0)
    feat_local = tots[0].shape[0]
    peers = out.shape[0]
    first = lax.axis_index("feat") * feat_local
    for rr in range(CHUNK):
        r = step * CHUNK + rr
        g = grow[pl.ds(r, 1), :].astype(BF16)
        n = cnt[r, 0]
        for s in range(blk.shape[1]):
            t = jnp.dot(g, blk[rr, s], preferred_element_type=F32)
            t = jnp.where(s < n, t, 0.0)
            tot = tots[s % len(tots)]
            c = col[r, s] - first
            tot[pl.ds(c, 1), :] += t

    @pl.when(step == pl.num_programs(0) - 1)
    def _():
        tile = spread(square[0:1, 0:1])

        def put(d, carry):
            at = pl.ds(pl.multiple_of(d * own, own), own)
            acc = tots[0][at, :]
            for tot in tots[1:]:
                acc = acc + tot[at, :]
            out[d, 0:own, :] = acc.astype(BF16)
            out[d, own : own + META, :] = tile
            return carry

        lax.fori_loop(0, peers, put, 0)


def clear(own, tots, peers):
    def zero(d, carry):
        at = pl.ds(pl.multiple_of(d * own, own), own)
        for tot in tots:
            tot[at, :] = jnp.zeros((own, 128), F32)
        return carry

    lax.fori_loop(0, peers, zero, 0)


def rhs_of(labels, weight):
    return weight[...] * (2 * labels[...] - 1).astype(F32)


def first_backward(own, col, cnt, labels, weight, blk, out, grow, square, *tots):
    @pl.when(pl.program_id(0) == 0)
    def _():
        resid = rhs_of(labels, weight)
        grow[...] = (weight[...] * resid).astype(BF16).astype(F32)
        square[...] = jnp.broadcast_to(total_sum(resid * resid), square.shape)
        clear(own, tots, out.shape[0])

    backward_steps(own, blk, col, cnt, grow, tots, out, square)


def next_backward(own, col, cnt, labels, weight, mine, other, scal, blk, out, resid_out, alpha_out, grow, square, *tots):
    @pl.when(pl.program_id(0) == 0)
    def _():
        rows = weight.shape[0]
        alpha = jnp.sqrt(gathered_sum(mine[rows:, :] + other[rows:, :]) + EPS)
        beta = scal[0:1, 0:1]
        unit = rhs_of(labels, weight) / beta
        resid = weight[...] * ((mine[0:rows, :] + other[0:rows, :]) / alpha) - alpha * unit
        resid_out[...] = resid
        alpha_out[...] = jnp.broadcast_to(alpha, alpha_out.shape)
        grow[...] = (weight[...] * resid).astype(BF16).astype(F32)
        square[...] = jnp.broadcast_to(total_sum(resid * resid), square.shape)
        clear(own, tots, out.shape[0])

    backward_steps(own, blk, col, cnt, grow, tots, out, square)


def reduced(own, recv):
    def add(d, carry):
        acc, meta = carry
        return acc + recv[d, 0:own, :].astype(F32), meta + recv[d, own : own + META, :].astype(F32)

    acc, meta = lax.fori_loop(
        0, recv.shape[0], add, (jnp.zeros((own, 128), F32), jnp.zeros((META, 128), F32)), unroll=8
    )
    return acc, jnp.sqrt(gathered_sum(meta) + EPS)


def send_step(own, out, step_vec):
    data = step_vec.astype(BF16)
    tile = spread(total_sum(step_vec * step_vec))

    def put(d, carry):
        out[d, 0:own, :] = data
        out[d, own : own + META, :] = tile
        return carry

    lax.fori_loop(0, out.shape[0], put, 0, unroll=8)


def first_owner(own, recv, scale_hbm, out, step_out, beta_out, scale, sem):
    start = pl.multiple_of(lax.axis_index("rows") * own, own)
    copy = pltpu.make_async_copy(scale_hbm.at[pl.ds(start, own), :], scale, sem)
    copy.start()
    total, beta = reduced(own, recv)
    copy.wait()
    step_vec = scale[...] * total / beta
    step_out[...] = step_vec
    beta_out[...] = jnp.broadcast_to(beta, beta_out.shape)
    send_step(own, out, step_vec)


def next_owner(own, recv, step_in, alpha_in, scale_hbm, out, beta_out, scale, sem):
    start = pl.multiple_of(lax.axis_index("rows") * own, own)
    copy = pltpu.make_async_copy(scale_hbm.at[pl.ds(start, own), :], scale, sem)
    copy.start()
    total, beta = reduced(own, recv)
    copy.wait()
    unit = step_in[...] / alpha_in[0:1, 0:1]
    step_vec = scale[...] * total / beta - beta * unit
    beta_out[...] = jnp.broadcast_to(beta, beta_out.shape)
    send_step(own, out, step_vec)


def forward(own, col, cnt, recv, scale, blk, out, table):
    step = pl.program_id(0)
    rows = out.shape[0] - META
    first = lax.axis_index("feat") * table.shape[0]

    @pl.when(step == 0)
    def _():
        def fill(d, meta):
            at = pl.ds(pl.multiple_of(d * own, own), own)
            scaled = scale[at, :] * recv[d, 0:own, :].astype(F32)
            table[at, :] = scaled.astype(BF16).astype(F32)
            return meta + recv[d, own : own + META, :].astype(F32)

        out[rows:, :] = lax.fori_loop(0, recv.shape[0], fill, jnp.zeros((META, 128), F32))

    for rr in range(CHUNK):
        r = step * CHUNK + rr
        n = cnt[r, 0]
        acc = jnp.zeros((1, 128), F32)
        for s in range(blk.shape[1]):
            c = col[r, s] - first
            v = jnp.where(s < n, table[pl.ds(c, 1), :], 0.0).astype(BF16)
            acc = acc + lax.dot_general(v, blk[rr, s], (((1,), (1,)), ((), ())), preferred_element_type=F32)
        out[pl.ds(r, 1), :] = acc


def last_rows(labels, weight, mine, other, resid_in, alpha_in, beta_in, resid_out, alpha_out, out):
    del labels
    rows = weight.shape[0]
    alpha = jnp.sqrt(gathered_sum(mine[rows:, :] + other[rows:, :]) + EPS)
    unit = resid_in[...] / beta_in[0:1, 0:1]
    resid = weight[...] * ((mine[0:rows, :] + other[0:rows, :]) / alpha) - alpha * unit
    resid_out[...] = resid
    alpha_out[...] = jnp.broadcast_to(alpha, alpha_out.shape)
    out[...] = jnp.broadcast_to(total_sum(resid * resid), out.shape)


def combine(own, recv0, recv1, squares, beta0, alpha0, beta1, alpha1, out):
    b0, a0 = beta0[0:1, 0:1], alpha0[0:1, 0:1]
    b1, a1 = beta1[0:1, 0:1], alpha1[0:1, 0:1]
    b2 = jnp.sqrt(jnp.sum(squares[...], axis=0, keepdims=True)[:, 0:1] + EPS)
    rho1 = jnp.sqrt(a0 * a0 + b1 * b1)
    cos1, sin1 = a0 / rho1, b1 / rho1
    theta1, bar1 = sin1 * a1, -cos1 * a1
    phi1, phibar1 = cos1 * b0, sin1 * b0
    rho2 = jnp.sqrt(bar1 * bar1 + b2 * b2)
    phi2 = (bar1 / rho2) * phibar1
    second = phi2 / rho2
    first = phi1 / rho1 - second * (theta1 / rho1)
    first, second = first / a0, second / a1
    for d in range(recv0.shape[0]):
        out[d * own : (d + 1) * own, :] = first * recv0[d, 0:own, :].astype(F32) + second * recv1[d, 0:own, :].astype(F32)


def body(blocks, col_index, row_counts, labels, row_weight, feature_scale):
    rows, slots, side, _ = blocks.shape
    feat_local = feature_scale.shape[0]
    peers = lax.axis_size("rows")
    own = feat_local // peers
    steps = rows // CHUNK
    smem = pl.BlockSpec(memory_space=pltpu.SMEM)
    vmem = pl.BlockSpec(memory_space=pltpu.VMEM)
    hbm = pl.BlockSpec(memory_space=pl.ANY)

    def whole(*shape):
        return pl.BlockSpec(shape, lambda i: (0,) * len(shape))

    blk = pl.BlockSpec((CHUNK, slots, side, side), lambda i: (i, 0, 0, 0))
    small = jax.ShapeDtypeStruct((8, 128), F32)
    rowvec = jax.ShapeDtypeStruct((rows, side), F32)
    packet = jax.ShapeDtypeStruct((peers, own + META, side), BF16)
    part = jax.ShapeDtypeStruct((rows + META, side), F32)
    params = pltpu.CompilerParams(vmem_limit_bytes=40 << 20)
    scratch = [pltpu.VMEM((rows, side), F32), pltpu.VMEM((8, 128), F32)]
    scratch += [pltpu.VMEM((feat_local, side), F32)] * slots
    scale_scratch = [pltpu.VMEM((own, side), F32), pltpu.SemaphoreType.DMA]

    def exchange(x):
        return lax.all_to_all(x, "rows", 0, 0)

    def swap(x):
        return lax.ppermute(x, "feat", [(0, 1), (1, 0)])

    def forward_part(recv):
        return pl.pallas_call(
            functools.partial(forward, own),
            grid=(steps,),
            out_shape=part,
            in_specs=[smem, smem, whole(*packet.shape), whole(feat_local, side), blk],
            out_specs=whole(*part.shape),
            scratch_shapes=[pltpu.VMEM((feat_local, side), F32)],
            compiler_params=params,
            name="forward",
        )(col_index, row_counts, recv, feature_scale, blocks)

    send = pl.pallas_call(
        functools.partial(first_backward, own),
        grid=(steps,),
        out_shape=packet,
        in_specs=[smem, smem, whole(rows, side), whole(rows, side), blk],
        out_specs=whole(*packet.shape),
        scratch_shapes=scratch,
        compiler_params=params,
        name="backward0",
    )(col_index, row_counts, labels, row_weight, blocks)
    send, step0, beta0 = pl.pallas_call(
        functools.partial(first_owner, own),
        out_shape=(packet, jax.ShapeDtypeStruct((own, side), F32), small),
        in_specs=[vmem, hbm],
        out_specs=(vmem, vmem, vmem),
        scratch_shapes=scale_scratch,
        compiler_params=params,
        name="owner0",
    )(exchange(send), feature_scale)
    recv0 = exchange(send)
    mine = forward_part(recv0)
    send, resid1, alpha0 = pl.pallas_call(
        functools.partial(next_backward, own),
        grid=(steps,),
        out_shape=(packet, rowvec, small),
        in_specs=[smem, smem, whole(rows, side), whole(rows, side), whole(*part.shape), whole(*part.shape), whole(8, 128), blk],
        out_specs=(whole(*packet.shape), whole(rows, side), whole(8, 128)),
        scratch_shapes=scratch,
        compiler_params=params,
        name="backward1",
    )(col_index, row_counts, labels, row_weight, mine, swap(mine), beta0, blocks)
    send, beta1 = pl.pallas_call(
        functools.partial(next_owner, own),
        out_shape=(packet, small),
        in_specs=[vmem, vmem, vmem, hbm],
        out_specs=(vmem, vmem),
        scratch_shapes=scale_scratch,
        compiler_params=params,
        name="owner1",
    )(exchange(send), step0, alpha0, feature_scale)
    recv1 = exchange(send)
    mine = forward_part(recv1)
    resid2, alpha1, send = pl.pallas_call(
        last_rows,
        out_shape=(rowvec, small, jax.ShapeDtypeStruct((peers, side), F32)),
        in_specs=[vmem] * 7,
        out_specs=(vmem, vmem, vmem),
        compiler_params=params,
        name="last_rows",
    )(labels, row_weight, mine, swap(mine), resid1, alpha0, beta1)
    solution = pl.pallas_call(
        functools.partial(combine, own),
        out_shape=jax.ShapeDtypeStruct((feat_local, side), F32),
        in_specs=[vmem] * 7,
        out_specs=vmem,
        compiler_params=params,
        name="combine",
    )(recv0, recv1, exchange(send), beta0, alpha0, beta1, alpha1)
    return (solution, resid2)


def solution(mesh):
    return jax.shard_map(
        body,
        mesh=mesh,
        in_specs=(
            P("rows", "feat", None, None),
            P("rows", "feat"),
            P("rows", "feat"),
            P("rows", None),
            P("rows", None),
            P("feat", None),
        ),
        out_specs=(P("feat", None), P("rows", None)),
        check_vma=False,
    )
```

```python
import functools

import jax
import jax.numpy as jnp
from jax import lax
from jax.experimental import pallas as pl
from jax.experimental.pallas import tpu as pltpu
from jax.sharding import PartitionSpec as P

F32 = jnp.float32
BF16 = jnp.bfloat16
EPS = 1e-06
META = 8
UNROLL = 16
PHASES = 4
COPIES = 32
LIST = 640
TABLES = 4


def spread(value):
    full = jnp.broadcast_to(value, (META, 128))
    high = full.astype(BF16).astype(F32)
    rest = full - high
    mid = rest.astype(BF16).astype(F32)
    low = (rest - mid).astype(BF16).astype(F32)
    row = lax.broadcasted_iota(jnp.int32, (META, 128), 0)
    tile = jnp.where(row == 0, high, jnp.where(row == 1, mid, jnp.where(row == 2, low, 0.0)))
    return tile.astype(BF16)


def total_sum(x):
    return jnp.sum(jnp.sum(x, axis=0, keepdims=True), axis=1, keepdims=True)


def gathered_sum(tile):
    return jnp.sum(tile, axis=0, keepdims=True)[:, 0:1]


def build_list(col, cnt, codes, first):
    slots, rows = col.shape
    pad = rows << 12
    at = 0
    for p in range(PHASES):

        def row(r, k):
            n = cnt[0, r]
            for s in range(slots):
                codes[k] = (col[s, r] - first) | (r << 12) | ((r * slots + s) << 20)
                k = k + (s < n).astype(jnp.int32)
            return k

        at = lax.fori_loop(p * (rows // PHASES), (p + 1) * (rows // PHASES), row, at)
        for u in range(UNROLL):
            codes[at + u] = pad
        at = ((at + UNROLL - 1) // UNROLL) * UNROLL
        codes[LIST - 1 - p] = at


def decode(code):
    return code & 4095, (code >> 12) & 255, code >> 20


def tile_row(ref, i):
    return jnp.broadcast_to(ref[i >> 3, pl.ds(i & 7, 1), :], (8, 128))


def left_operand(parts, split):
    row = lax.broadcasted_iota(jnp.int32, (8, 128), 0)
    place = row & 3 if split else row
    halves = []
    for a, b in parts:
        x = jnp.where(place == a[0], a[1], jnp.where(place == b[0], b[1], 0.0))
        if split:
            high = x.astype(BF16).astype(F32)
            x = jnp.where(row < 4, high, x - high)
        halves.append(x.astype(BF16))
    return jnp.concatenate(halves, axis=1)


def right_operand(blk, e):
    top = jnp.concatenate([blk[e[0]], blk[e[1]]], axis=1)
    low = jnp.concatenate([blk[e[2]], blk[e[3]]], axis=1)
    return jnp.concatenate([top, low], axis=0)


def pick(t, m, half, split):
    lanes = slice(half * 128, half * 128 + 128)
    return t[m : m + 1, lanes] + t[m + 4 : m + 5, lanes] if split else t[m : m + 1, lanes]


def add_row(ref, i, value):
    ref[i >> 3, pl.ds(i & 7, 1), :] += value


def backward_range(codes, blk, grow, tots, begin, end, split):
    def some(i, carry):
        for q in range(UNROLL // 4):
            at = i * UNROLL + q * 4
            c, r, e = zip(*[decode(codes[at + u]) for u in range(4)])
            g = [tile_row(grow, r[u]) for u in range(4)]
            lhs = left_operand([((0, g[0]), (1, g[1])), ((2, g[2]), (3, g[3]))], split)
            t = jnp.dot(lhs, right_operand(blk, e), preferred_element_type=F32)
            for u in range(4):
                add_row(tots[u], c[u], pick(t, u, u & 1, split))
        return carry

    lax.fori_loop(begin // UNROLL, end // UNROLL, some, 0)


def forward_range(codes, blk, table, outs, begin, end):
    def some(i, carry):
        for q in range(UNROLL // 4):
            at = i * UNROLL + q * 4
            c, r, e = zip(*[decode(codes[at + u]) for u in range(4)])
            v = [tile_row(table, c[u]) for u in range(4)]
            lhs = left_operand([((0, v[0]), (2, v[2])), ((1, v[1]), (3, v[3]))], False)
            t = lax.dot_general(lhs, right_operand(blk, e), (((1,), (1,)), ((), ())), preferred_element_type=F32)
            for u in range(4):
                add_row(outs[u], r[u], pick(t, u, u >> 1, False))
        return carry

    lax.fori_loop(begin // UNROLL, end // UNROLL, some, 0)


def clear(refs):
    def zero(d, carry):
        for ref in refs:
            for u in range(8):
                ref[d * 8 + u] = jnp.zeros((8, 128), F32)
        return carry

    lax.fori_loop(0, refs[0].shape[0] // 8, zero, 0)


def set_rows(grow, value):
    rows = value.shape[0]
    grow[0 : rows // 8] = value.reshape(rows // 8, 8, 128)
    grow[rows // 8 :] = jnp.zeros((grow.shape[0] - rows // 8, 8, 128), F32)


def send_partials(own, tots, square, out):
    tile = spread(square)
    tiles = own // 8

    def put(d, carry):
        at = pl.ds(d * tiles, tiles)
        acc = tots[0][at]
        for tot in tots[1:]:
            acc = acc + tot[at]
        out[d, 0:own, :] = acc.reshape(own, 128).astype(BF16)
        out[d, own : own + META, :] = tile
        return carry

    lax.fori_loop(0, out.shape[0], put, 0)


def rhs_of(labels, weight):
    return weight[...] * (2 * labels[...] - 1).astype(F32)


def first_backward(own, col, cnt, labels_hbm, weight_hbm, blocks, out, held, codes, labels, weight, grow, sems, row_sems, *tots):
    slots = col.shape[0]
    each = held.shape[0] // COPIES
    copies = [
        pltpu.make_async_copy(blocks.at[pl.ds(i * each, each)], held.at[pl.ds(i * each, each)], sems.at[i]) for i in range(COPIES)
    ]
    small = [
        pltpu.make_async_copy(labels_hbm, labels, row_sems.at[0]),
        pltpu.make_async_copy(weight_hbm, weight, row_sems.at[1]),
    ]
    for copy in small + copies:
        copy.start()
    build_list(col, cnt, codes, lax.axis_index("feat") * (tots[0].shape[0] * 8))
    clear(tots)
    for copy in small:
        copy.wait()
    resid = rhs_of(labels, weight)
    set_rows(grow, (weight[...] * resid).astype(BF16).astype(F32))
    begin = 0
    for p in range(PHASES):
        for copy in copies[p * (COPIES // PHASES) : (p + 1) * (COPIES // PHASES)]:
            copy.wait()
        end = codes[LIST - 1 - p]
        backward_range(codes, held, grow, tots, begin, end, False)
        begin = end
    send_partials(own, tots, total_sum(resid * resid), out)


def next_backward(own, codes, labels, weight, mine, other, beta_in, held, out, resid_out, alpha_out, grow, *tots):
    rows = weight.shape[0]
    clear(tots)
    alpha = jnp.sqrt(gathered_sum(mine[rows:, :] + other[rows:, :]) + EPS)
    unit = rhs_of(labels, weight) / beta_in[0:1, 0:1]
    resid = weight[...] * ((mine[0:rows, :] + other[0:rows, :]) / alpha) - alpha * unit
    resid_out[...] = resid
    alpha_out[...] = jnp.broadcast_to(alpha, alpha_out.shape)
    set_rows(grow, weight[...] * resid)
    backward_range(codes, held, grow, tots, 0, codes[LIST - PHASES], True)
    send_partials(own, tots, total_sum(resid * resid), out)


def reduced(own, recv):
    def add(d, carry):
        acc, meta = carry
        return acc + recv[d, 0:own, :].astype(F32), meta + recv[d, own : own + META, :].astype(F32)

    acc, meta = lax.fori_loop(
        0, recv.shape[0], add, (jnp.zeros((own, 128), F32), jnp.zeros((META, 128), F32)), unroll=8
    )
    return acc, jnp.sqrt(gathered_sum(meta) + EPS)


def send_step(own, out, step_vec, scale):
    data = (scale * step_vec).astype(BF16)
    tile = spread(total_sum(step_vec * step_vec))

    def put(d, carry):
        out[d, 0:own, :] = data
        out[d, own : own + META, :] = tile
        return carry

    lax.fori_loop(0, out.shape[0], put, 0, unroll=8)


def first_owner(own, recv, scale_hbm, out, step_out, beta_out, scale, sem):
    start = pl.multiple_of(lax.axis_index("rows") * own, own)
    copy = pltpu.make_async_copy(scale_hbm.at[pl.ds(start, own), :], scale, sem)
    copy.start()
    total, beta = reduced(own, recv)
    copy.wait()
    step_vec = scale[...] * total / beta
    step_out[...] = step_vec
    beta_out[...] = jnp.broadcast_to(beta, beta_out.shape)
    send_step(own, out, step_vec, scale[...])


def next_owner(own, recv, step_in, alpha_in, scale_hbm, out, beta_out, scale, sem):
    start = pl.multiple_of(lax.axis_index("rows") * own, own)
    copy = pltpu.make_async_copy(scale_hbm.at[pl.ds(start, own), :], scale, sem)
    copy.start()
    total, beta = reduced(own, recv)
    copy.wait()
    unit = step_in[...] / alpha_in[0:1, 0:1]
    step_vec = scale[...] * total / beta - beta * unit
    beta_out[...] = jnp.broadcast_to(beta, beta_out.shape)
    send_step(own, out, step_vec, scale[...])


def forward(own, codes, recv, held, out, table, *outs):
    rows = out.shape[0] - META
    tiles = own // 8

    def fill(d, meta):
        table[pl.ds(d * tiles, tiles)] = recv[d, 0:own, :].astype(F32).reshape(tiles, 8, 128)
        return meta + recv[d, own : own + META, :].astype(F32)

    out[rows:, :] = lax.fori_loop(0, recv.shape[0], fill, jnp.zeros((META, 128), F32))
    for ref in outs:
        ref[...] = jnp.zeros_like(ref)
    forward_range(codes, held, table, outs, 0, codes[LIST - PHASES])
    acc = outs[0][0 : rows // 8]
    for ref in outs[1:]:
        acc = acc + ref[0 : rows // 8]
    out[0:rows, :] = acc.reshape(rows, 128)


def last_rows(weight, mine, other, resid_in, beta_in, resid_out, alpha_out, out):
    rows = weight.shape[0]
    alpha = jnp.sqrt(gathered_sum(mine[rows:, :] + other[rows:, :]) + EPS)
    unit = resid_in[...] / beta_in[0:1, 0:1]
    resid = weight[...] * ((mine[0:rows, :] + other[0:rows, :]) / alpha) - alpha * unit
    resid_out[...] = resid
    alpha_out[...] = jnp.broadcast_to(alpha, alpha_out.shape)
    out[...] = jnp.broadcast_to(total_sum(resid * resid), out.shape)


def combine(own, recv0, recv1, scale, squares, beta0, alpha0, beta1, alpha1, out):
    b0, a0 = beta0[0:1, 0:1], alpha0[0:1, 0:1]
    b1, a1 = beta1[0:1, 0:1], alpha1[0:1, 0:1]
    b2 = jnp.sqrt(jnp.sum(squares[...], axis=0, keepdims=True)[:, 0:1] + EPS)
    rho1 = jnp.sqrt(a0 * a0 + b1 * b1)
    cos1, sin1 = a0 / rho1, b1 / rho1
    theta1, bar1 = sin1 * a1, -cos1 * a1
    phi1, phibar1 = cos1 * b0, sin1 * b0
    rho2 = jnp.sqrt(bar1 * bar1 + b2 * b2)
    phi2 = (bar1 / rho2) * phibar1
    second = phi2 / rho2
    first = phi1 / rho1 - second * (theta1 / rho1)
    first, second = first / a0, second / a1

    def put(d, carry):
        at = pl.ds(pl.multiple_of(d * own, own), own)
        mixed = first * recv0[d, 0:own, :].astype(F32) + second * recv1[d, 0:own, :].astype(F32)
        out[at, :] = mixed / scale[at, :]
        return carry

    lax.fori_loop(0, recv0.shape[0], put, 0, unroll=2)


def body(blocks, col_index, row_counts, labels, row_weight, feature_scale):
    rows, slots, side, _ = blocks.shape
    feat_local = feature_scale.shape[0]
    peers = lax.axis_size("rows")
    own = feat_local // peers
    far = [pltpu.with_memory_space_constraint(x, pltpu.HBM) for x in (col_index.T, row_counts.T, labels, row_weight)]
    far_blocks = pltpu.with_memory_space_constraint(blocks.reshape(rows * slots, side, side), pltpu.HBM)
    smem = pl.BlockSpec(memory_space=pltpu.SMEM)
    vmem = pl.BlockSpec(memory_space=pltpu.VMEM)
    hbm = pl.BlockSpec(memory_space=pltpu.HBM)
    small = jax.ShapeDtypeStruct((8, 128), F32)
    rowvec = jax.ShapeDtypeStruct((rows, side), F32)
    packet = jax.ShapeDtypeStruct((peers, own + META, side), BF16)
    part = jax.ShapeDtypeStruct((rows + META, side), F32)
    params = pltpu.CompilerParams(vmem_limit_bytes=20 << 20)
    tables = [pltpu.VMEM((feat_local // 8, 8, side), F32)] * TABLES
    row_table = pltpu.VMEM((rows // 8 + 1, 8, side), F32)
    scale_scratch = [pltpu.VMEM((own, side), F32), pltpu.SemaphoreType.DMA]

    def exchange(x):
        return lax.all_to_all(x, "rows", 0, 0)

    def swap(x):
        return lax.ppermute(x, "feat", [(0, 1), (1, 0)])

    def forward_part(recv):
        return pl.pallas_call(
            functools.partial(forward, own),
            out_shape=part,
            in_specs=[smem, vmem, vmem],
            out_specs=vmem,
            scratch_shapes=[tables[0]] + [row_table] * TABLES,
            compiler_params=params,
            name="forward",
        )(codes, recv, held)

    send, held, codes = pl.pallas_call(
        functools.partial(first_backward, own),
        out_shape=(packet, pltpu.VMEM((rows * slots, side, side), BF16), jax.ShapeDtypeStruct((LIST,), jnp.int32)),
        in_specs=[smem, smem, hbm, hbm, hbm],
        out_specs=(vmem, vmem, smem),
        scratch_shapes=[
            pltpu.VMEM((rows, side), jnp.int32),
            pltpu.VMEM((rows, side), F32),
            row_table,
            pltpu.SemaphoreType.DMA((COPIES,)),
            pltpu.SemaphoreType.DMA((2,)),
        ]
        + tables,
        compiler_params=params,
        name="backward0",
    )(*far, far_blocks)
    send, step0, beta0 = pl.pallas_call(
        functools.partial(first_owner, own),
        out_shape=(packet, jax.ShapeDtypeStruct((own, side), F32), small),
        in_specs=[vmem, hbm],
        out_specs=(vmem, vmem, vmem),
        scratch_shapes=scale_scratch,
        compiler_params=params,
        name="owner0",
    )(exchange(send), feature_scale)
    recv0 = exchange(send)
    mine = forward_part(recv0)
    send, resid1, alpha0 = pl.pallas_call(
        functools.partial(next_backward, own),
        out_shape=(packet, rowvec, small),
        in_specs=[smem] + [vmem] * 6,
        out_specs=(vmem, vmem, vmem),
        scratch_shapes=[row_table] + tables,
        compiler_params=params,
        name="backward1",
    )(codes, labels, row_weight, mine, swap(mine), beta0, held)
    send, beta1 = pl.pallas_call(
        functools.partial(next_owner, own),
        out_shape=(packet, small),
        in_specs=[vmem, vmem, vmem, hbm],
        out_specs=(vmem, vmem),
        scratch_shapes=scale_scratch,
        compiler_params=params,
        name="owner1",
    )(exchange(send), step0, alpha0, feature_scale)
    recv1 = exchange(send)
    mine = forward_part(recv1)
    resid2, alpha1, send = pl.pallas_call(
        last_rows,
        out_shape=(rowvec, small, jax.ShapeDtypeStruct((peers, side), F32)),
        in_specs=[vmem] * 5,
        out_specs=(vmem, vmem, vmem),
        compiler_params=params,
        name="last_rows",
    )(row_weight, mine, swap(mine), resid1, beta1)
    solution = pl.pallas_call(
        functools.partial(combine, own),
        out_shape=jax.ShapeDtypeStruct((feat_local, side), F32),
        in_specs=[vmem] * 8,
        out_specs=vmem,
        compiler_params=params,
        name="combine",
    )(recv0, recv1, feature_scale, exchange(send), beta0, alpha0, beta1, alpha1)
    return (solution, resid2)


def solution(mesh):
    return jax.shard_map(
        body,
        mesh=mesh,
        in_specs=(
            P("rows", "feat", None, None),
            P("rows", "feat"),
            P("rows", "feat"),
            P("rows", None),
            P("rows", None),
            P("feat", None),
        ),
        out_specs=(P("feat", None), P("rows", None)),
        check_vma=False,
    )
```

```python
import functools

import jax
import jax.numpy as jnp
from jax import lax
from jax.experimental import pallas as pl
from jax.experimental.pallas import tpu as pltpu
from jax.sharding import PartitionSpec as P

F32 = jnp.float32
BF16 = jnp.bfloat16
EPS = 1e-06
ITERS = 2
META = 8
UNROLL = 32
COPIES = 32
EARLY = 8
LIST = 640
TABLES = 4
PACKET = 32
ROOM = PACKET - 1
RAISED = 128.0


def spread(value):
    full = jnp.broadcast_to(value, (META, 128))
    high = full.astype(BF16).astype(F32)
    rest = full - high
    mid = rest.astype(BF16).astype(F32)
    low = (rest - mid).astype(BF16).astype(F32)
    row = lax.broadcasted_iota(jnp.int32, (META, 128), 0)
    tile = jnp.where(row == 0, high, jnp.where(row == 1, mid, jnp.where(row == 2, low, 0.0)))
    return tile.astype(BF16)


def total_sum(x):
    return jnp.sum(jnp.sum(x, axis=0, keepdims=True), axis=1, keepdims=True)


def gathered_sum(tile):
    return jnp.sum(tile, axis=0, keepdims=True)[:, 0:1]


def decode(code):
    return code & 4095, (code >> 12) & 255, code >> 20


def tile_row(ref, i):
    return jnp.broadcast_to(ref[i >> 3, pl.ds(i & 7, 1), :], (8, 128))


def left_operand(parts, split):
    row = lax.broadcasted_iota(jnp.int32, (8, 128), 0)
    place = row & 3 if split else row
    halves = []
    for a, b in parts:
        x = jnp.where(place == a[0], a[1], jnp.where(place == b[0], b[1], 0.0))
        if split:
            high = x.astype(BF16).astype(F32)
            x = jnp.where(row < 4, high, x - high)
        halves.append(x.astype(BF16))
    return jnp.concatenate(halves, axis=1)


def right_operand(blk, e):
    top = jnp.concatenate([blk[e[0]], blk[e[1]]], axis=1)
    low = jnp.concatenate([blk[e[2]], blk[e[3]]], axis=1)
    return jnp.concatenate([top, low], axis=0)


def pick(t, m, half, split):
    lanes = slice(half * 128, half * 128 + 128)
    return t[m : m + 1, lanes] + t[m + 4 : m + 5, lanes] if split else t[m : m + 1, lanes]


def put_row(ref, i, value):
    ref[i >> 3, pl.ds(i & 7, 1), :] = value


def add_row(ref, i, value):
    ref[i >> 3, pl.ds(i & 7, 1), :] += value


def backward_list(codes, blk, grow, stage):
    def some(i, carry):
        for q in range(UNROLL // 4):
            at = i * UNROLL + q * 4
            c, r, e = zip(*[decode(codes[at + u]) for u in range(4)])
            g = [tile_row(grow, r[u]) for u in range(4)]
            lhs = left_operand([((0, g[0]), (1, g[1])), ((2, g[2]), (3, g[3]))], True)
            t = jnp.dot(lhs, right_operand(blk, e), preferred_element_type=F32)
            for u in range(4):
                put_row(stage, c[u], pick(t, u, u & 1, True))
        return carry

    lax.fori_loop(0, codes[LIST - 1] // UNROLL, some, 0)


def forward_list(codes, blk, table, outs):
    def some(i, carry):
        for q in range(UNROLL // 4):
            at = i * UNROLL + q * 4
            c, r, e = zip(*[decode(codes[at + u]) for u in range(4)])
            v = [tile_row(table, c[u]) for u in range(4)]
            lhs = left_operand([((0, v[0]), (2, v[2])), ((1, v[1]), (3, v[3]))], False)
            t = lax.dot_general(lhs, right_operand(blk, e), (((1,), (1,)), ((), ())), preferred_element_type=F32)
            for u in range(4):
                add_row(outs[u], r[u], pick(t, u, u >> 1, False))
        return carry

    lax.fori_loop(0, codes[LIST - 1] // UNROLL, some, 0)


def clear(ref):
    def zero(d, carry):
        ref[d] = jnp.zeros((8, 128), F32)
        return carry

    lax.fori_loop(0, ref.shape[0], zero, 0, unroll=8)


def set_rows(grow, value):
    rows = value.shape[0]
    grow[0 : rows // 8] = value.reshape(rows // 8, 8, 128)
    grow[rows // 8 :] = jnp.zeros((grow.shape[0] - rows // 8, 8, 128), F32)


def quarter():
    lane = lax.broadcasted_iota(jnp.int32, (8, 128), 1) // (128 // 4)
    return (lane - lax.axis_index("rows")) & 3


def send_partials(stage, index, meta, square, flag, out):
    part = quarter()
    lane = lax.broadcasted_iota(jnp.int32, (8, 128), 1)
    three = spread(square).astype(F32)
    sums = jnp.where(part == 1, three[0:1, :], jnp.where(part == 2, three[1:2, :], three[2:3, :]))
    raised = (part == 0) & (lane % PACKET == ROOM)
    for d in range(index.shape[0]):
        meta[d] = jnp.where(part != 0, sums, jnp.where(raised, flag, index[d]))
    tiles = PACKET // 8
    last = lax.broadcasted_iota(jnp.int32, (PACKET, 128), 0) == ROOM

    def put(d, carry):
        row = jnp.broadcast_to(meta[d >> 3, pl.ds(d & 7, 1), :], (PACKET, 128))
        rows = stage[pl.ds(d * tiles, tiles)].reshape(PACKET, 128)
        out[d] = jnp.where(last, row, rows).astype(BF16)
        return carry

    lax.fori_loop(0, out.shape[0], put, 0, unroll=4)


def rhs_of(labels, weight):
    return weight[...] * (2 * labels[...] - 1).astype(F32)


def place_entries(own, peers, cols, counts, places, index):
    slots, rows = cols.shape
    first = lax.axis_index("feat") * (own * peers)
    lane0 = (lax.axis_index("rows") & 3) * PACKET
    owner_id = lax.broadcasted_iota(jnp.int32, (peers, rows), 0)
    down = lax.broadcasted_iota(jnp.int32, (rows, rows), 0)
    earlier = jnp.where(down < lax.broadcasted_iota(jnp.int32, (rows, rows), 1), 1.0, 0.0).astype(BF16)
    before = jnp.zeros((peers, 1), F32)
    meta = jnp.zeros((peers, rows), F32)
    for s in range(slots):
        c = cols[s : s + 1, :] - first
        owner = lax.shift_right_logical(c, own.bit_length() - 1)
        live = s < counts[...]
        hit = jnp.where((owner_id == owner) & live, 1.0, 0.0)
        rank = before + jnp.dot(hit.astype(BF16), earlier, preferred_element_type=F32)
        before = before + jnp.sum(hit, axis=1, keepdims=True)
        rank = jnp.sum(hit * rank, axis=0, keepdims=True).astype(jnp.int32)
        fits = live & (rank < ROOM)
        places[s : s + 1, :] = jnp.where(fits, owner * PACKET + rank, peers * PACKET)
        lane = jnp.where(fits, rank + lane0, -1)
        known = ((c & (own - 1)) + 1).astype(F32)
        spot = jnp.where(down == lane, 1.0, 0.0).astype(BF16)
        meta = meta + lax.dot_general(
            (hit * known).astype(BF16), spot, (((1,), (1,)), ((), ())), preferred_element_type=F32
        )
    index[...] = meta.reshape(index.shape)
    return jnp.where(jnp.max(before, axis=0, keepdims=True) > ROOM, RAISED, 0.0)


def first_backward(
    own, col_hbm, cnt_hbm, labels_hbm, weight_hbm, blocks, out, held, forth, back, index,
    cols, counts, col, cnt, places, labels, weight, wide, place_tile, stage, meta, sems, small_sems,
):
    slots, rows = cols.shape
    each = held.shape[0] // COPIES
    per_step = 8 * slots // each
    first = lax.axis_index("feat") * (own * out.shape[0])

    def block_copy(i):
        at = pl.ds(i * each, each)
        return pltpu.make_async_copy(blocks.at[at], held.at[at], sems.at[i])

    pairs = ((col_hbm, cols), (cnt_hbm, counts), (labels_hbm, labels), (weight_hbm, weight), (col_hbm, col), (cnt_hbm, cnt))
    small = [pltpu.make_async_copy(src, dst, small_sems.at[i]) for i, (src, dst) in enumerate(pairs)]
    for copy in small:
        copy.start()
    for i in range(EARLY):
        block_copy(i).start()
    clear(stage)
    for copy in small:
        copy.wait()
    flag = place_entries(own, out.shape[0], cols, counts, place_tile, index)
    to_scalars = pltpu.make_async_copy(place_tile, places, small_sems.at[len(pairs)])
    to_scalars.start(priority=1)
    for i in range(EARLY, COPIES):
        block_copy(i).start()
    resid = rhs_of(labels, weight)
    rowed = (weight[...] * resid).astype(BF16).astype(F32)
    odd = lax.broadcasted_iota(jnp.int32, rowed.shape, 0) & 1
    wide[:, 0:128] = jnp.where(odd == 0, rowed, 0.0)
    wide[:, 128:256] = jnp.where(odd == 1, rowed, 0.0)
    to_scalars.wait()

    def step(p, k):
        r0 = pl.multiple_of(p * 8, 8)
        for i in range(per_step):
            block_copy(p * per_step + i).wait()
        lhs = wide[pl.ds(r0, 8), :].astype(BF16)
        for pair in range(4):
            for h in range(slots // 2):
                e = [(r0 + 2 * pair + q) * slots + 2 * h + s for q in range(2) for s in range(2)]
                t = jnp.dot(lhs, right_operand(held, e), preferred_element_type=F32)
                for u in range(4):
                    m, slot = 2 * pair + u // 2, 2 * h + u % 2
                    r = r0 + m
                    place = places[slot, r]
                    put_row(stage, place, pick(t, m, u % 2, False))
                    code = (r << 12) | (e[u] << 20)
                    forth[k] = code | (col[slot, r] - first)
                    back[k] = code | place
                    k = k + (slot < cnt[0, r]).astype(jnp.int32)
        return k

    live = lax.fori_loop(0, rows // 8, step, 0)
    for u in range(UNROLL):
        forth[live + u] = rows << 12
        back[live + u] = (rows << 12) | (out.shape[0] * PACKET)
    end = ((live + UNROLL - 1) // UNROLL) * UNROLL
    forth[LIST - 1] = end
    back[LIST - 1] = end
    send_partials(stage, index, meta, total_sum(resid * resid), flag, out)


def next_backward(codes, labels, weight, mine, other, scal, index, held, out, resid_out, scal_out, grow, stage, meta):
    rows = weight.shape[0]
    clear(stage)
    both = mine[rows:, :] + other[rows:, :]
    alpha = jnp.sqrt(gathered_sum(both[0:3, :]) + EPS)
    unit = rhs_of(labels, weight) / scal[0:1, 0:1]
    resid = weight[...] * ((mine[0:rows, :] + other[0:rows, :]) / alpha) - alpha * unit
    resid_out[...] = resid
    scal_out[...] = pair_tile(alpha, both[3:4, 0:1])
    set_rows(grow, weight[...] * resid)
    backward_list(codes, held, grow, stage)
    send_partials(stage, index, meta, total_sum(resid * resid), 0.0, out)


def pair_tile(a, b):
    row = lax.broadcasted_iota(jnp.int32, (8, 128), 0)
    return jnp.where(row == 0, jnp.broadcast_to(a, (8, 128)), jnp.broadcast_to(b, (8, 128)))


def reduced(own, recv):
    lane = lax.broadcasted_iota(jnp.int32, (1, 128), 1) // PACKET
    feature = (lax.broadcasted_iota(jnp.int32, (own, 128), 0) + 1).astype(F32)
    acc = jnp.zeros((own, 128), F32)
    sums = jnp.zeros((1, 128), F32)
    most = jnp.zeros((1, 128), F32)
    for g in range(recv.shape[0] // 4):
        known = jnp.zeros((1, 128), F32)
        for j in range(4):
            row = recv[4 * g + j, PACKET - 8 : PACKET, :].astype(F32)[7:8, :]
            known = known + jnp.where(lane == j, row, 0.0)
            sums = sums + jnp.where(lane == j, 0.0, row)
        most = jnp.maximum(most, known)
        chosen = jnp.where(feature == known, 1.0, 0.0).astype(BF16)
        acc = acc + jnp.dot(chosen, recv[4 * g : 4 * g + 4].reshape(128, 128), preferred_element_type=F32)
    first = lax.broadcasted_iota(jnp.int32, (1, 128), 1) % PACKET == 0
    total = jnp.sum(jnp.where(first, sums, 0.0), axis=1, keepdims=True)
    return acc, jnp.sqrt(total + EPS), jnp.max(most, axis=1, keepdims=True)


def send_step(own, out, step_vec, scale):
    data = (scale * step_vec).astype(BF16)
    tile = spread(total_sum(step_vec * step_vec))

    def put(d, carry):
        out[d, 0:own, :] = data
        out[d, own : own + META, :] = tile
        return carry

    lax.fori_loop(0, out.shape[0], put, 0, unroll=8)


def first_owner(own, recv, scale_hbm, out, step_out, beta_out, scale, sem):
    start = pl.multiple_of(lax.axis_index("rows") * own, own)
    copy = pltpu.make_async_copy(scale_hbm.at[pl.ds(start, own), :], scale, sem)
    copy.start()
    total, beta, most = reduced(own, recv)
    copy.wait()
    step_vec = scale[...] * total / beta
    step_out[...] = step_vec
    beta_out[...] = pair_tile(beta, jnp.where(most > own, 1.0, 0.0))
    send_step(own, out, step_vec, scale[...])


def next_owner(own, recv, step_in, alpha_in, scale_hbm, out, beta_out, scale, sem):
    start = pl.multiple_of(lax.axis_index("rows") * own, own)
    copy = pltpu.make_async_copy(scale_hbm.at[pl.ds(start, own), :], scale, sem)
    copy.start()
    total, beta, _ = reduced(own, recv)
    copy.wait()
    unit = step_in[...] / alpha_in[0:1, 0:1]
    step_vec = scale[...] * total / beta - beta * unit
    beta_out[...] = jnp.broadcast_to(beta, beta_out.shape)
    send_step(own, out, step_vec, scale[...])


def forward(own, codes, recv, scal, held, out, table, *outs):
    rows = out.shape[0] - META
    tiles = own // 8

    def fill(d, meta):
        table[pl.ds(d * tiles, tiles)] = recv[d, 0:own, :].astype(F32).reshape(tiles, 8, 128)
        return meta + recv[d, own : own + META, :].astype(F32)

    meta = lax.fori_loop(0, recv.shape[0], fill, jnp.zeros((META, 128), F32), unroll=2)
    row = lax.broadcasted_iota(jnp.int32, (META, 128), 0)
    out[rows:, :] = jnp.where(row == 3, scal[1:2, :], meta)
    for ref in outs:
        ref[...] = jnp.zeros_like(ref)
    forward_list(codes, held, table, outs)
    acc = outs[0][0 : rows // 8]
    for ref in outs[1:]:
        acc = acc + ref[0 : rows // 8]
    out[0:rows, :] = acc.reshape(rows, 128)


def last_rows(weight, mine, other, resid_in, beta_in, resid_out, alpha_out, out):
    rows = weight.shape[0]
    both = mine[rows:, :] + other[rows:, :]
    alpha = jnp.sqrt(gathered_sum(both[0:3, :]) + EPS)
    unit = resid_in[...] / beta_in[0:1, 0:1]
    resid = weight[...] * ((mine[0:rows, :] + other[0:rows, :]) / alpha) - alpha * unit
    resid_out[...] = resid
    alpha_out[...] = jnp.broadcast_to(alpha, alpha_out.shape)
    out[...] = jnp.broadcast_to(total_sum(resid * resid), out.shape)


def combine(own, recv0, recv1, scale, squares, beta0, alpha0, beta1, alpha1, out_hbm, flag, out, sems):
    b0, a0 = beta0[0:1, 0:1], alpha0[0:1, 0:1]
    b1, a1 = beta1[0:1, 0:1], alpha1[0:1, 0:1]
    b2 = jnp.sqrt(jnp.sum(squares[...], axis=0, keepdims=True)[:, 0:1] + EPS)
    rho1 = jnp.sqrt(a0 * a0 + b1 * b1)
    cos1, sin1 = a0 / rho1, b1 / rho1
    theta1, bar1 = sin1 * a1, -cos1 * a1
    phi1, phibar1 = cos1 * b0, sin1 * b0
    rho2 = jnp.sqrt(bar1 * bar1 + b2 * b2)
    phi2 = (bar1 / rho2) * phibar1
    second = phi2 / rho2
    first = phi1 / rho1 - second * (theta1 / rho1)
    first, second = first / a0, second / a1
    flag[...] = jnp.broadcast_to(alpha0[1:2, :], flag.shape)
    n = sems.shape[0]
    each = out.shape[0] // n

    def copy(i):
        at = pl.ds(pl.multiple_of(i * each, each), each)
        return pltpu.make_async_copy(out.at[at], out_hbm.at[at], sems.at[i])

    def put(i, carry):
        for j in range(each // own):
            d = i * (each // own) + j
            at = pl.ds(pl.multiple_of(d * own, own), own)
            mixed = first * recv0[d, 0:own, :].astype(F32) + second * recv1[d, 0:own, :].astype(F32)
            out[at, :] = mixed / scale[at, :]
        copy(i).start()
        return carry

    lax.fori_loop(0, n, put, 0)
    lax.fori_loop(0, n, lambda i, carry: (copy(i).wait(), carry)[1], 0)


def general(blocks, col_index, row_counts, labels, row_weight, feature_scale):
    feat_local, side = feature_scale.shape
    peers = lax.axis_size("rows")
    local_col = col_index - lax.axis_index("feat") * feat_local
    live = (lax.broadcasted_iota(jnp.int32, col_index.shape, 1) < row_counts).astype(F32)

    def over_rows(x):
        return jnp.sum(lax.all_to_all(jnp.broadcast_to(x, (peers, 8, 128)), "rows", 0, 0), axis=0)[0, 0]

    def over_feat(x):
        return x + lax.ppermute(x, "feat", [(0, 1), (1, 0)])

    def backward(resid):
        rowed = (row_weight * resid).astype(BF16)
        terms = jnp.einsum("rsij,ri->rsj", blocks, rowed, preferred_element_type=F32) * live[:, :, None]
        partial = jax.ops.segment_sum(terms.reshape(-1, side), local_col.reshape(-1), num_segments=feat_local)
        owned = jnp.sum(lax.all_to_all(partial.reshape(peers, -1, side), "rows", 0, 0), axis=0)
        total = lax.all_to_all(jnp.broadcast_to(owned, (peers,) + owned.shape), "rows", 0, 0).reshape(feat_local, side)
        return total, jnp.sqrt(over_rows(jnp.sum(resid * resid)) + EPS)

    def norm(step_vec):
        return jnp.sqrt(over_feat(jnp.full((8, 128), jnp.sum(step_vec * step_vec)))[0, 0] + EPS)

    resid = row_weight * (2 * labels - 1).astype(F32)
    total, beta = backward(resid)
    step_vec = feature_scale * total / beta
    alpha = norm(step_vec)
    unit_feat = step_vec / alpha
    start = (resid, beta, alpha, unit_feat, beta, alpha, unit_feat, jnp.zeros_like(unit_feat))

    def iteration(_, state):
        resid, beta, alpha, unit_feat, phi_bar, rho_bar, search, result = state
        scaled = (feature_scale * unit_feat).astype(BF16)
        picked = jnp.take(scaled, local_col, axis=0)
        terms = jnp.einsum("rsij,rsj->rsi", blocks, picked, preferred_element_type=F32)
        resid = row_weight * over_feat(jnp.sum(terms * live[:, :, None], axis=1)) - alpha * (resid / beta)
        total, beta = backward(resid)
        step_vec = feature_scale * total / beta - beta * unit_feat
        alpha = norm(step_vec)
        unit_feat = step_vec / alpha
        rho = jnp.sqrt(rho_bar * rho_bar + beta * beta)
        cosine, sine = rho_bar / rho, beta / rho
        theta, rho_bar = sine * alpha, -cosine * alpha
        phi, phi_bar = cosine * phi_bar, sine * phi_bar
        result = result + phi / rho * search
        search = unit_feat - theta / rho * search
        return (resid, beta, alpha, unit_feat, phi_bar, rho_bar, search, result)

    state = lax.fori_loop(0, ITERS, iteration, start)
    return state[-1], state[0]


def body(blocks, col_index, row_counts, labels, row_weight, feature_scale):
    rows, slots, side, _ = blocks.shape
    feat_local = feature_scale.shape[0]
    peers = lax.axis_size("rows")
    own = feat_local // peers
    far = [pltpu.with_memory_space_constraint(x, pltpu.HBM) for x in (col_index.T, row_counts.T, labels, row_weight)]
    far_blocks = pltpu.with_memory_space_constraint(blocks.reshape(rows * slots, side, side), pltpu.HBM)
    smem = pl.BlockSpec(memory_space=pltpu.SMEM)
    vmem = pl.BlockSpec(memory_space=pltpu.VMEM)
    hbm = pl.BlockSpec(memory_space=pltpu.HBM)
    small = jax.ShapeDtypeStruct((8, 128), F32)
    rowvec = jax.ShapeDtypeStruct((rows, side), F32)
    packet = jax.ShapeDtypeStruct((peers, own + META, side), BF16)
    sparse = jax.ShapeDtypeStruct((peers, PACKET, side), BF16)
    part = jax.ShapeDtypeStruct((rows + META, side), F32)
    listed = jax.ShapeDtypeStruct((LIST,), jnp.int32)
    marked = jax.ShapeDtypeStruct((peers // 8, 8, side), F32)
    params = pltpu.CompilerParams(vmem_limit_bytes=20 << 20)
    table = pltpu.VMEM((feat_local // 8, 8, side), F32)
    stage = pltpu.VMEM((peers * PACKET // 8 + 1, 8, side), F32)
    mark = pltpu.VMEM(marked.shape, F32)
    row_table = pltpu.VMEM((rows // 8 + 1, 8, side), F32)
    scale_scratch = [pltpu.VMEM((own, side), F32), pltpu.SemaphoreType.DMA]

    def exchange(x):
        return lax.all_to_all(x, "rows", 0, 0)

    def swap(x):
        return lax.ppermute(x, "feat", [(0, 1), (1, 0)])

    def forward_part(recv, scal):
        return pl.pallas_call(
            functools.partial(forward, own),
            out_shape=part,
            in_specs=[smem, vmem, vmem, vmem],
            out_specs=vmem,
            scratch_shapes=[table] + [row_table] * TABLES,
            compiler_params=params,
            name="forward",
        )(forth, recv, scal, held)

    send, held, forth, back, index = pl.pallas_call(
        functools.partial(first_backward, own),
        out_shape=(
            sparse,
            pltpu.VMEM((rows * slots, side, side), BF16),
            listed,
            listed,
            marked,
        ),
        in_specs=[hbm] * 5,
        out_specs=(vmem, vmem, smem, smem, vmem),
        scratch_shapes=[
            pltpu.VMEM((slots, rows), jnp.int32),
            pltpu.VMEM((1, rows), jnp.int32),
            pltpu.SMEM((slots, rows), jnp.int32),
            pltpu.SMEM((1, rows), jnp.int32),
            pltpu.SMEM((slots, rows), jnp.int32),
            pltpu.VMEM((rows, side), jnp.int32),
            pltpu.VMEM((rows, side), F32),
            pltpu.VMEM((rows, 2 * side), F32),
            pltpu.VMEM((slots, rows), jnp.int32),
            stage,
            mark,
            pltpu.SemaphoreType.DMA((COPIES,)),
            pltpu.SemaphoreType.DMA((7,)),
        ],
        compiler_params=params,
        name="backward0",
    )(*far, far_blocks)
    send, step0, beta0 = pl.pallas_call(
        functools.partial(first_owner, own),
        out_shape=(packet, jax.ShapeDtypeStruct((own, side), F32), small),
        in_specs=[vmem, hbm],
        out_specs=(vmem, vmem, vmem),
        scratch_shapes=scale_scratch,
        compiler_params=params,
        name="owner0",
    )(exchange(send), feature_scale)
    recv0 = exchange(send)
    mine = forward_part(recv0, beta0)
    send, resid1, alpha0 = pl.pallas_call(
        next_backward,
        out_shape=(sparse, rowvec, small),
        in_specs=[smem] + [vmem] * 7,
        out_specs=(vmem, vmem, vmem),
        scratch_shapes=[row_table, stage, mark],
        compiler_params=params,
        name="backward1",
    )(back, labels, row_weight, mine, swap(mine), beta0, index, held)
    send, beta1 = pl.pallas_call(
        functools.partial(next_owner, own),
        out_shape=(packet, small),
        in_specs=[vmem, vmem, vmem, hbm],
        out_specs=(vmem, vmem),
        scratch_shapes=scale_scratch,
        compiler_params=params,
        name="owner1",
    )(exchange(send), step0, alpha0, feature_scale)
    recv1 = exchange(send)
    mine = forward_part(recv1, beta0)
    resid2, alpha1, send = pl.pallas_call(
        last_rows,
        out_shape=(rowvec, small, jax.ShapeDtypeStruct((peers, side), F32)),
        in_specs=[vmem] * 5,
        out_specs=(vmem, vmem, vmem),
        compiler_params=params,
        name="last_rows",
    )(row_weight, mine, swap(mine), resid1, beta1)
    result, flag = pl.pallas_call(
        functools.partial(combine, own),
        out_shape=(jax.ShapeDtypeStruct((feat_local, side), F32), small),
        in_specs=[vmem] * 8,
        out_specs=(hbm, vmem),
        scratch_shapes=[pltpu.VMEM((feat_local, side), F32), pltpu.SemaphoreType.DMA((16,))],
        compiler_params=params,
        name="combine",
    )(recv0, recv1, feature_scale, exchange(send), beta0, alpha0, beta1, alpha1)

    def fits(state):
        return state[0] > 0.0

    def again(state):
        args = (blocks, col_index, row_counts, labels, row_weight, feature_scale)
        return (jnp.zeros_like(state[0]),) + general(*lax.optimization_barrier((state[0],) + args)[1:])

    _, result, resid2 = lax.while_loop(fits, again, (flag[0, 0], result, resid2))
    return (result, resid2)


def solution(mesh):
    return jax.shard_map(
        body,
        mesh=mesh,
        in_specs=(
            P("rows", "feat", None, None),
            P("rows", "feat"),
            P("rows", "feat"),
            P("rows", None),
            P("rows", None),
            P("feat", None),
        ),
        out_specs=(P("feat", None), P("rows", None)),
        check_vma=False,
    )
```

```python
import functools

import jax
import jax.numpy as jnp
from jax import lax
from jax.experimental import pallas as pl
from jax.experimental.pallas import tpu as pltpu
from jax.sharding import PartitionSpec as P

F32 = jnp.float32
BF16 = jnp.bfloat16
EPS = 1e-06
ITERS = 2
META = 8
UNROLL = 64
COPIES = 32
EARLY = 8
LIST = 640
TABLES = 4
PACKET = 32
ROOM = PACKET - 1
RAISED = 128.0


def spread(value):
    full = jnp.broadcast_to(value, (META, 128))
    high = full.astype(BF16).astype(F32)
    rest = full - high
    mid = rest.astype(BF16).astype(F32)
    low = (rest - mid).astype(BF16).astype(F32)
    row = lax.broadcasted_iota(jnp.int32, (META, 128), 0)
    tile = jnp.where(row == 0, high, jnp.where(row == 1, mid, jnp.where(row == 2, low, 0.0)))
    return tile.astype(BF16)


def total_sum(x):
    return jnp.sum(jnp.sum(x, axis=0, keepdims=True), axis=1, keepdims=True)


def gathered_sum(tile):
    return jnp.sum(tile, axis=0, keepdims=True)[:, 0:1]


def decode(code):
    return code & 4095, (code >> 12) & 255, code >> 20


def tile_row(ref, i):
    return jnp.broadcast_to(ref[i >> 3, pl.ds(i & 7, 1), :], (8, 128))


def left_operand(parts, split):
    row = lax.broadcasted_iota(jnp.int32, (8, 128), 0)
    place = row & 3 if split else row
    halves = []
    for a, b in parts:
        x = jnp.where(place == a[0], a[1], jnp.where(place == b[0], b[1], 0.0))
        if split:
            high = x.astype(BF16).astype(F32)
            x = jnp.where(row < 4, high, x - high)
        halves.append(x.astype(BF16))
    return jnp.concatenate(halves, axis=1)


def right_operand(blk, e):
    top = jnp.concatenate([blk[e[0]], blk[e[1]]], axis=1)
    low = jnp.concatenate([blk[e[2]], blk[e[3]]], axis=1)
    return jnp.concatenate([top, low], axis=0)


def pick(t, m, half, split):
    lanes = slice(half * 128, half * 128 + 128)
    return t[m : m + 1, lanes] + t[m + 4 : m + 5, lanes] if split else t[m : m + 1, lanes]


def put_row(ref, i, value):
    ref[i >> 3, pl.ds(i & 7, 1), :] = value


def add_row(ref, i, value):
    ref[i >> 3, pl.ds(i & 7, 1), :] += value


def backward_list(codes, blk, grow, stage):
    def some(i, carry):
        for q in range(UNROLL // 4):
            at = i * UNROLL + q * 4
            c, r, e = zip(*[decode(codes[at + u]) for u in range(4)])
            g = [tile_row(grow, r[u]) for u in range(4)]
            lhs = left_operand([((0, g[0]), (1, g[1])), ((2, g[2]), (3, g[3]))], True)
            t = jnp.dot(lhs, right_operand(blk, e), preferred_element_type=F32)
            for u in range(4):
                put_row(stage, c[u], pick(t, u, u & 1, True))
        return carry

    lax.fori_loop(0, codes[LIST - 1] // UNROLL, some, 0)


def forward_list(codes, blk, table, outs):
    def some(i, carry):
        for q in range(UNROLL // 4):
            at = i * UNROLL + q * 4
            c, r, e = zip(*[decode(codes[at + u]) for u in range(4)])
            v = [tile_row(table, c[u]) for u in range(4)]
            lhs = left_operand([((0, v[0]), (2, v[2])), ((1, v[1]), (3, v[3]))], False)
            t = lax.dot_general(lhs, right_operand(blk, e), (((1,), (1,)), ((), ())), preferred_element_type=F32)
            for u in range(4):
                add_row(outs[u], r[u], pick(t, u, u >> 1, False))
        return carry

    lax.fori_loop(0, codes[LIST - 1] // UNROLL, some, 0)


def clear(ref):
    def zero(d, carry):
        ref[d] = jnp.zeros((8, 128), F32)
        return carry

    lax.fori_loop(0, ref.shape[0], zero, 0, unroll=8)


def set_rows(grow, value):
    rows = value.shape[0]
    grow[0 : rows // 8] = value.reshape(rows // 8, 8, 128)
    grow[rows // 8 :] = jnp.zeros((grow.shape[0] - rows // 8, 8, 128), F32)


def quarter():
    lane = lax.broadcasted_iota(jnp.int32, (8, 128), 1) // (128 // 4)
    return (lane - lax.axis_index("rows")) & 3


def send_partials(stage, index, meta, square, flag, out):
    part = quarter()
    lane = lax.broadcasted_iota(jnp.int32, (8, 128), 1)
    three = spread(square).astype(F32)
    sums = jnp.where(part == 1, three[0:1, :], jnp.where(part == 2, three[1:2, :], three[2:3, :]))
    raised = (part == 0) & (lane % PACKET == ROOM)
    for d in range(index.shape[0]):
        meta[d] = jnp.where(part != 0, sums, jnp.where(raised, flag, index[d]))
    tiles = PACKET // 8
    last = lax.broadcasted_iota(jnp.int32, (PACKET, 128), 0) == ROOM

    def put(d, carry):
        row = jnp.broadcast_to(meta[d >> 3, pl.ds(d & 7, 1), :], (PACKET, 128))
        rows = stage[pl.ds(d * tiles, tiles)].reshape(PACKET, 128)
        out[d] = jnp.where(last, row, rows).astype(BF16)
        return carry

    lax.fori_loop(0, out.shape[0], put, 0, unroll=4)


def rhs_of(labels, weight):
    return weight[...] * (2 * labels[...] - 1).astype(F32)


def place_entries(own, peers, cols, counts, places, index):
    slots, rows = cols.shape
    first = lax.axis_index("feat") * (own * peers)
    lane0 = (lax.axis_index("rows") & 3) * PACKET
    owner_id = lax.broadcasted_iota(jnp.int32, (peers, rows), 0)
    down = lax.broadcasted_iota(jnp.int32, (rows, rows), 0)
    earlier = jnp.where(down < lax.broadcasted_iota(jnp.int32, (rows, rows), 1), 1.0, 0.0).astype(BF16)
    before = jnp.zeros((peers, 1), F32)
    meta = jnp.zeros((peers, rows), F32)
    for s in range(slots):
        c = cols[s : s + 1, :] - first
        owner = lax.shift_right_logical(c, own.bit_length() - 1)
        live = s < counts[...]
        hit = jnp.where((owner_id == owner) & live, 1.0, 0.0)
        rank = before + jnp.dot(hit.astype(BF16), earlier, preferred_element_type=F32)
        before = before + jnp.sum(hit, axis=1, keepdims=True)
        rank = jnp.sum(hit * rank, axis=0, keepdims=True).astype(jnp.int32)
        fits = live & (rank < ROOM)
        places[s : s + 1, :] = jnp.where(fits, owner * PACKET + rank, peers * PACKET)
        lane = jnp.where(fits, rank + lane0, -1)
        known = ((c & (own - 1)) + 1).astype(F32)
        spot = jnp.where(down == lane, 1.0, 0.0).astype(BF16)
        meta = meta + lax.dot_general(
            (hit * known).astype(BF16), spot, (((1,), (1,)), ((), ())), preferred_element_type=F32
        )
    index[...] = meta.reshape(index.shape)
    return jnp.where(jnp.max(before, axis=0, keepdims=True) > ROOM, RAISED, 0.0)


def first_backward(
    own, col_hbm, cnt_hbm, labels_hbm, weight_hbm, blocks, out, held, forth, back, index,
    cols, counts, col, cnt, places, labels, weight, wide, place_tile, stage, meta, sems, small_sems,
):
    slots, rows = cols.shape
    each = held.shape[0] // COPIES
    per_step = 8 * slots // each
    first = lax.axis_index("feat") * (own * out.shape[0])

    def block_copy(i):
        at = pl.ds(i * each, each)
        return pltpu.make_async_copy(blocks.at[at], held.at[at], sems.at[i])

    pairs = ((col_hbm, cols), (cnt_hbm, counts), (labels_hbm, labels), (weight_hbm, weight), (col_hbm, col), (cnt_hbm, cnt))
    small = [pltpu.make_async_copy(src, dst, small_sems.at[i]) for i, (src, dst) in enumerate(pairs)]
    for copy in small:
        copy.start()
    for i in range(EARLY):
        block_copy(i).start()
    clear(stage)
    for copy in small:
        copy.wait()
    flag = place_entries(own, out.shape[0], cols, counts, place_tile, index)
    to_scalars = pltpu.make_async_copy(place_tile, places, small_sems.at[len(pairs)])
    to_scalars.start(priority=1)
    for i in range(EARLY, COPIES):
        block_copy(i).start()
    resid = rhs_of(labels, weight)
    rowed = (weight[...] * resid).astype(BF16).astype(F32)
    odd = lax.broadcasted_iota(jnp.int32, rowed.shape, 0) & 1
    wide[:, 0:128] = jnp.where(odd == 0, rowed, 0.0)
    wide[:, 128:256] = jnp.where(odd == 1, rowed, 0.0)
    to_scalars.wait()

    def step(p, k):
        r0 = pl.multiple_of(p * 8, 8)
        for i in range(per_step):
            block_copy(p * per_step + i).wait()
        lhs = wide[pl.ds(r0, 8), :].astype(BF16)
        for pair in range(4):
            for h in range(slots // 2):
                e = [(r0 + 2 * pair + q) * slots + 2 * h + s for q in range(2) for s in range(2)]
                t = jnp.dot(lhs, right_operand(held, e), preferred_element_type=F32)
                for u in range(4):
                    m, slot = 2 * pair + u // 2, 2 * h + u % 2
                    r = r0 + m
                    place = places[slot, r]
                    put_row(stage, place, pick(t, m, u % 2, False))
                    code = (r << 12) | (e[u] << 20)
                    forth[k] = code | (col[slot, r] - first)
                    back[k] = code | place
                    k = k + (slot < cnt[0, r]).astype(jnp.int32)
        return k

    live = lax.fori_loop(0, rows // 8, step, 0)
    for u in range(UNROLL):
        forth[live + u] = rows << 12
        back[live + u] = (rows << 12) | (out.shape[0] * PACKET)
    end = ((live + UNROLL - 1) // UNROLL) * UNROLL
    forth[LIST - 1] = end
    back[LIST - 1] = end
    send_partials(stage, index, meta, total_sum(resid * resid), flag, out)


def next_backward(codes, labels, weight, mine, other, scal, index, held, out, resid_out, scal_out, grow, stage, meta):
    rows = weight.shape[0]
    clear(stage)
    both = mine[rows:, :] + other[rows:, :]
    alpha = jnp.sqrt(gathered_sum(both[0:3, :]) + EPS)
    unit = rhs_of(labels, weight) / scal[0:1, 0:1]
    resid = weight[...] * ((mine[0:rows, :] + other[0:rows, :]) / alpha) - alpha * unit
    resid_out[...] = resid
    scal_out[...] = pair_tile(alpha, both[3:4, 0:1])
    set_rows(grow, weight[...] * resid)
    backward_list(codes, held, grow, stage)
    send_partials(stage, index, meta, total_sum(resid * resid), 0.0, out)


def pair_tile(a, b):
    row = lax.broadcasted_iota(jnp.int32, (8, 128), 0)
    return jnp.where(row == 0, jnp.broadcast_to(a, (8, 128)), jnp.broadcast_to(b, (8, 128)))


def reduced(own, recv):
    lane = lax.broadcasted_iota(jnp.int32, (1, 128), 1) // PACKET
    feature = (lax.broadcasted_iota(jnp.int32, (own, 128), 0) + 1).astype(F32)
    acc = jnp.zeros((own, 128), F32)
    sums = jnp.zeros((1, 128), F32)
    most = jnp.zeros((1, 128), F32)
    for g in range(recv.shape[0] // 4):
        known = jnp.zeros((1, 128), F32)
        for j in range(4):
            row = recv[4 * g + j, PACKET - 8 : PACKET, :].astype(F32)[7:8, :]
            known = known + jnp.where(lane == j, row, 0.0)
            sums = sums + jnp.where(lane == j, 0.0, row)
        most = jnp.maximum(most, known)
        chosen = jnp.where(feature == known, 1.0, 0.0).astype(BF16)
        acc = acc + jnp.dot(chosen, recv[4 * g : 4 * g + 4].reshape(128, 128), preferred_element_type=F32)
    first = lax.broadcasted_iota(jnp.int32, (1, 128), 1) % PACKET == 0
    total = jnp.sum(jnp.where(first, sums, 0.0), axis=1, keepdims=True)
    return acc, jnp.sqrt(total + EPS), jnp.max(most, axis=1, keepdims=True)


def send_step(own, out, step_vec, scale):
    data = (scale * step_vec).astype(BF16)
    tile = spread(total_sum(step_vec * step_vec))

    def put(d, carry):
        out[d, 0:own, :] = data
        out[d, own : own + META, :] = tile
        return carry

    lax.fori_loop(0, out.shape[0], put, 0, unroll=8)


def first_owner(own, recv, scale_hbm, out, step_out, beta_out, scale, sem):
    start = pl.multiple_of(lax.axis_index("rows") * own, own)
    copy = pltpu.make_async_copy(scale_hbm.at[pl.ds(start, own), :], scale, sem)
    copy.start()
    total, beta, most = reduced(own, recv)
    copy.wait()
    step_vec = scale[...] * total / beta
    step_out[...] = step_vec
    beta_out[...] = pair_tile(beta, jnp.where(most > own, 1.0, 0.0))
    send_step(own, out, step_vec, scale[...])


def next_owner(own, recv, step_in, alpha_in, scale_hbm, out, beta_out, scale, sem):
    start = pl.multiple_of(lax.axis_index("rows") * own, own)
    copy = pltpu.make_async_copy(scale_hbm.at[pl.ds(start, own), :], scale, sem)
    copy.start()
    total, beta, _ = reduced(own, recv)
    copy.wait()
    unit = step_in[...] / alpha_in[0:1, 0:1]
    step_vec = scale[...] * total / beta - beta * unit
    beta_out[...] = jnp.broadcast_to(beta, beta_out.shape)
    send_step(own, out, step_vec, scale[...])


def forward(own, codes, recv, scal, held, out, table, *outs):
    rows = out.shape[0] - META
    tiles = own // 8

    def fill(d, meta):
        table[pl.ds(d * tiles, tiles)] = recv[d, 0:own, :].astype(F32).reshape(tiles, 8, 128)
        return meta + recv[d, own : own + META, :].astype(F32)

    meta = lax.fori_loop(0, recv.shape[0], fill, jnp.zeros((META, 128), F32), unroll=2)
    row = lax.broadcasted_iota(jnp.int32, (META, 128), 0)
    out[rows:, :] = jnp.where(row == 3, scal[1:2, :], meta)
    for ref in outs:
        ref[...] = jnp.zeros_like(ref)
    forward_list(codes, held, table, outs)
    acc = outs[0][0 : rows // 8]
    for ref in outs[1:]:
        acc = acc + ref[0 : rows // 8]
    out[0:rows, :] = acc.reshape(rows, 128)


def last_rows(weight, mine, other, resid_in, beta_in, resid_out, alpha_out, out):
    rows = weight.shape[0]
    both = mine[rows:, :] + other[rows:, :]
    alpha = jnp.sqrt(gathered_sum(both[0:3, :]) + EPS)
    unit = resid_in[...] / beta_in[0:1, 0:1]
    resid = weight[...] * ((mine[0:rows, :] + other[0:rows, :]) / alpha) - alpha * unit
    resid_out[...] = resid
    alpha_out[...] = jnp.broadcast_to(alpha, alpha_out.shape)
    out[...] = jnp.broadcast_to(total_sum(resid * resid), out.shape)


def combine(own, recv0, recv1, scale, squares, beta0, alpha0, beta1, alpha1, out_hbm, flag, out, sems):
    b0, a0 = beta0[0:1, 0:1], alpha0[0:1, 0:1]
    b1, a1 = beta1[0:1, 0:1], alpha1[0:1, 0:1]
    b2 = jnp.sqrt(jnp.sum(squares[...], axis=0, keepdims=True)[:, 0:1] + EPS)
    rho1 = jnp.sqrt(a0 * a0 + b1 * b1)
    cos1, sin1 = a0 / rho1, b1 / rho1
    theta1, bar1 = sin1 * a1, -cos1 * a1
    phi1, phibar1 = cos1 * b0, sin1 * b0
    rho2 = jnp.sqrt(bar1 * bar1 + b2 * b2)
    phi2 = (bar1 / rho2) * phibar1
    second = phi2 / rho2
    first = phi1 / rho1 - second * (theta1 / rho1)
    first, second = first / a0, second / a1
    flag[0, 0] = jnp.max(alpha0[1:2, :])
    n = sems.shape[0]
    each = out.shape[0] // n

    def copy(i):
        at = pl.ds(pl.multiple_of(i * each, each), each)
        return pltpu.make_async_copy(out.at[at], out_hbm.at[at], sems.at[i])

    def put(i, carry):
        for j in range(each // own):
            d = i * (each // own) + j
            at = pl.ds(pl.multiple_of(d * own, own), own)
            mixed = first * recv0[d, 0:own, :].astype(F32) + second * recv1[d, 0:own, :].astype(F32)
            out[at, :] = mixed / scale[at, :]
        copy(i).start()
        return carry

    lax.fori_loop(0, n, put, 0)
    lax.fori_loop(0, n, lambda i, carry: (copy(i).wait(), carry)[1], 0)


def general(blocks, col_index, row_counts, labels, row_weight, feature_scale):
    feat_local, side = feature_scale.shape
    peers = lax.axis_size("rows")
    local_col = col_index.T - lax.axis_index("feat") * feat_local
    live = (lax.broadcasted_iota(jnp.int32, local_col.shape, 0) < row_counts.T).astype(F32)

    def over_rows(x):
        return jnp.sum(lax.all_to_all(jnp.broadcast_to(x, (peers, 8, 128)), "rows", 0, 0), axis=0)[0, 0]

    def over_feat(x):
        return x + lax.ppermute(x, "feat", [(0, 1), (1, 0)])

    def backward(resid):
        rowed = (row_weight * resid).astype(BF16)
        terms = jnp.einsum("rsij,ri->srj", blocks, rowed, preferred_element_type=F32) * live[:, :, None]
        partial = jax.ops.segment_sum(terms.reshape(-1, side), local_col.reshape(-1), num_segments=feat_local)
        owned = jnp.sum(lax.all_to_all(partial.reshape(peers, -1, side), "rows", 0, 0), axis=0)
        total = lax.all_to_all(jnp.broadcast_to(owned, (peers,) + owned.shape), "rows", 0, 0).reshape(feat_local, side)
        return total, jnp.sqrt(over_rows(jnp.sum(resid * resid)) + EPS)

    def norm(step_vec):
        return jnp.sqrt(over_feat(jnp.full((8, 128), jnp.sum(step_vec * step_vec)))[0, 0] + EPS)

    resid = row_weight * (2 * labels - 1).astype(F32)
    total, beta = backward(resid)
    step_vec = feature_scale * total / beta
    alpha = norm(step_vec)
    unit_feat = step_vec / alpha
    start = (resid, beta, alpha, unit_feat, beta, alpha, unit_feat, jnp.zeros_like(unit_feat))

    def iteration(_, state):
        resid, beta, alpha, unit_feat, phi_bar, rho_bar, search, result = state
        scaled = (feature_scale * unit_feat).astype(BF16)
        picked = jnp.take(scaled, local_col, axis=0)
        terms = jnp.einsum("rsij,srj->sri", blocks, picked, preferred_element_type=F32)
        resid = row_weight * over_feat(jnp.sum(terms * live[:, :, None], axis=0)) - alpha * (resid / beta)
        total, beta = backward(resid)
        step_vec = feature_scale * total / beta - beta * unit_feat
        alpha = norm(step_vec)
        unit_feat = step_vec / alpha
        rho = jnp.sqrt(rho_bar * rho_bar + beta * beta)
        cosine, sine = rho_bar / rho, beta / rho
        theta, rho_bar = sine * alpha, -cosine * alpha
        phi, phi_bar = cosine * phi_bar, sine * phi_bar
        result = result + phi / rho * search
        search = unit_feat - theta / rho * search
        return (resid, beta, alpha, unit_feat, phi_bar, rho_bar, search, result)

    state = lax.fori_loop(0, ITERS, iteration, start)
    return state[-1], state[0]


def body(blocks, col_index, row_counts, labels, row_weight, feature_scale):
    rows, slots, side, _ = blocks.shape
    feat_local = feature_scale.shape[0]
    peers = lax.axis_size("rows")
    own = feat_local // peers
    far = [pltpu.with_memory_space_constraint(x, pltpu.HBM) for x in (col_index.T, row_counts.T, labels, row_weight)]
    far_blocks = pltpu.with_memory_space_constraint(blocks.reshape(rows * slots, side, side), pltpu.HBM)
    smem = pl.BlockSpec(memory_space=pltpu.SMEM)
    vmem = pl.BlockSpec(memory_space=pltpu.VMEM)
    hbm = pl.BlockSpec(memory_space=pltpu.HBM)
    small = jax.ShapeDtypeStruct((8, 128), F32)
    rowvec = jax.ShapeDtypeStruct((rows, side), F32)
    packet = jax.ShapeDtypeStruct((peers, own + META, side), BF16)
    sparse = jax.ShapeDtypeStruct((peers, PACKET, side), BF16)
    part = jax.ShapeDtypeStruct((rows + META, side), F32)
    listed = jax.ShapeDtypeStruct((LIST,), jnp.int32)
    marked = jax.ShapeDtypeStruct((peers // 8, 8, side), F32)
    params = pltpu.CompilerParams(vmem_limit_bytes=20 << 20)
    table = pltpu.VMEM((feat_local // 8, 8, side), F32)
    stage = pltpu.VMEM((peers * PACKET // 8 + 1, 8, side), F32)
    mark = pltpu.VMEM(marked.shape, F32)
    row_table = pltpu.VMEM((rows // 8 + 1, 8, side), F32)
    scale_scratch = [pltpu.VMEM((own, side), F32), pltpu.SemaphoreType.DMA]

    def exchange(x):
        return lax.all_to_all(x, "rows", 0, 0)

    def swap(x):
        return lax.ppermute(x, "feat", [(0, 1), (1, 0)])

    def forward_part(recv, scal):
        return pl.pallas_call(
            functools.partial(forward, own),
            out_shape=part,
            in_specs=[smem, vmem, vmem, vmem],
            out_specs=vmem,
            scratch_shapes=[table] + [row_table] * TABLES,
            compiler_params=params,
            name="forward",
        )(forth, recv, scal, held)

    send, held, forth, back, index = pl.pallas_call(
        functools.partial(first_backward, own),
        out_shape=(
            sparse,
            pltpu.VMEM((rows * slots, side, side), BF16),
            listed,
            listed,
            marked,
        ),
        in_specs=[hbm] * 5,
        out_specs=(vmem, vmem, smem, smem, vmem),
        scratch_shapes=[
            pltpu.VMEM((slots, rows), jnp.int32),
            pltpu.VMEM((1, rows), jnp.int32),
            pltpu.SMEM((slots, rows), jnp.int32),
            pltpu.SMEM((1, rows), jnp.int32),
            pltpu.SMEM((slots, rows), jnp.int32),
            pltpu.VMEM((rows, side), jnp.int32),
            pltpu.VMEM((rows, side), F32),
            pltpu.VMEM((rows, 2 * side), F32),
            pltpu.VMEM((slots, rows), jnp.int32),
            stage,
            mark,
            pltpu.SemaphoreType.DMA((COPIES,)),
            pltpu.SemaphoreType.DMA((7,)),
        ],
        compiler_params=params,
        name="backward0",
    )(*far, far_blocks)
    send, step0, beta0 = pl.pallas_call(
        functools.partial(first_owner, own),
        out_shape=(packet, jax.ShapeDtypeStruct((own, side), F32), small),
        in_specs=[vmem, hbm],
        out_specs=(vmem, vmem, vmem),
        scratch_shapes=scale_scratch,
        compiler_params=params,
        name="owner0",
    )(exchange(send), feature_scale)
    recv0 = exchange(send)
    mine = forward_part(recv0, beta0)
    send, resid1, alpha0 = pl.pallas_call(
        next_backward,
        out_shape=(sparse, rowvec, small),
        in_specs=[smem] + [vmem] * 7,
        out_specs=(vmem, vmem, vmem),
        scratch_shapes=[row_table, stage, mark],
        compiler_params=params,
        name="backward1",
    )(back, labels, row_weight, mine, swap(mine), beta0, index, held)
    send, beta1 = pl.pallas_call(
        functools.partial(next_owner, own),
        out_shape=(packet, small),
        in_specs=[vmem, vmem, vmem, hbm],
        out_specs=(vmem, vmem),
        scratch_shapes=scale_scratch,
        compiler_params=params,
        name="owner1",
    )(exchange(send), step0, alpha0, feature_scale)
    recv1 = exchange(send)
    mine = forward_part(recv1, beta0)
    resid2, alpha1, send = pl.pallas_call(
        last_rows,
        out_shape=(rowvec, small, jax.ShapeDtypeStruct((peers, side), F32)),
        in_specs=[vmem] * 5,
        out_specs=(vmem, vmem, vmem),
        compiler_params=params,
        name="last_rows",
    )(row_weight, mine, swap(mine), resid1, beta1)
    result, flag = pl.pallas_call(
        functools.partial(combine, own),
        out_shape=(jax.ShapeDtypeStruct((feat_local, side), F32), jax.ShapeDtypeStruct((1, 1), F32)),
        in_specs=[vmem] * 8,
        out_specs=(hbm, smem),
        scratch_shapes=[pltpu.VMEM((feat_local, side), F32), pltpu.SemaphoreType.DMA((4,))],
        compiler_params=params,
        name="combine",
    )(recv0, recv1, feature_scale, exchange(send), beta0, alpha0, beta1, alpha1)

    def fits(state):
        return state[0] > 0.0

    def again(state):
        args = (blocks, col_index, row_counts, labels, row_weight, feature_scale)
        return (jnp.zeros_like(state[0]),) + general(*lax.optimization_barrier((state[0],) + args)[1:])

    _, result, resid2 = lax.while_loop(fits, again, (flag.reshape(()), result, resid2))
    return (result, resid2)


def solution(mesh):
    return jax.shard_map(
        body,
        mesh=mesh,
        in_specs=(
            P("rows", "feat", None, None),
            P("rows", "feat"),
            P("rows", "feat"),
            P("rows", None),
            P("rows", None),
            P("feat", None),
        ),
        out_specs=(P("feat", None), P("rows", None)),
        check_vma=False,
    )
```

```python
import functools

import jax
import jax.numpy as jnp
from jax import lax
from jax.experimental import pallas as pl
from jax.experimental.pallas import tpu as pltpu
from jax.sharding import PartitionSpec as P

F32 = jnp.float32
BF16 = jnp.bfloat16
EPS = 1e-06
ITERS = 2
META = 8
UNROLL = 64
COPIES = 16
EARLY = 1
LIST = 640
TABLES = 4
PACKET = 32
ROOM = PACKET - 1
RAISED = 128.0


def spread(value):
    full = jnp.broadcast_to(value, (META, 128))
    high = full.astype(BF16).astype(F32)
    rest = full - high
    mid = rest.astype(BF16).astype(F32)
    low = (rest - mid).astype(BF16).astype(F32)
    row = lax.broadcasted_iota(jnp.int32, (META, 128), 0)
    tile = jnp.where(row == 0, high, jnp.where(row == 1, mid, jnp.where(row == 2, low, 0.0)))
    return tile.astype(BF16)


def total_sum(x):
    return jnp.sum(jnp.sum(x, axis=0, keepdims=True), axis=1, keepdims=True)


def gathered_sum(tile):
    return jnp.sum(tile, axis=0, keepdims=True)[:, 0:1]


def decode(code):
    return code & 4095, (code >> 12) & 255, code >> 20


def tile_row(ref, i):
    return jnp.broadcast_to(ref[i >> 3, pl.ds(i & 7, 1), :], (8, 128))


def left_operand(parts, split):
    row = lax.broadcasted_iota(jnp.int32, (8, 128), 0)
    place = row & 3 if split else row
    halves = []
    for a, b in parts:
        x = jnp.where(place == a[0], a[1], jnp.where(place == b[0], b[1], 0.0))
        if split:
            high = x.astype(BF16).astype(F32)
            x = jnp.where(row < 4, high, x - high)
        halves.append(x.astype(BF16))
    return jnp.concatenate(halves, axis=1)


def right_operand(blk, e):
    top = jnp.concatenate([blk[e[0]], blk[e[1]]], axis=1)
    low = jnp.concatenate([blk[e[2]], blk[e[3]]], axis=1)
    return jnp.concatenate([top, low], axis=0)


def pick(t, m, half, split):
    lanes = slice(half * 128, half * 128 + 128)
    return t[m : m + 1, lanes] + t[m + 4 : m + 5, lanes] if split else t[m : m + 1, lanes]


def put_row(ref, i, value):
    ref[i >> 3, pl.ds(i & 7, 1), :] = value


def add_row(ref, i, value):
    ref[i >> 3, pl.ds(i & 7, 1), :] += value


def backward_list(codes, blk, grow, stage):
    def some(i, carry):
        for q in range(UNROLL // 4):
            at = i * UNROLL + q * 4
            c, r, e = zip(*[decode(codes[at + u]) for u in range(4)])
            g = [tile_row(grow, r[u]) for u in range(4)]
            lhs = left_operand([((0, g[0]), (1, g[1])), ((2, g[2]), (3, g[3]))], True)
            t = jnp.dot(lhs, right_operand(blk, e), preferred_element_type=F32)
            for u in range(4):
                put_row(stage, c[u], pick(t, u, u & 1, True))
        return carry

    lax.fori_loop(0, codes[LIST - 1] // UNROLL, some, 0)


def forward_list(codes, blk, table, outs):
    def some(i, carry):
        for q in range(UNROLL // 4):
            at = i * UNROLL + q * 4
            c, r, e = zip(*[decode(codes[at + u]) for u in range(4)])
            v = [tile_row(table, c[u]) for u in range(4)]
            lhs = left_operand([((0, v[0]), (2, v[2])), ((1, v[1]), (3, v[3]))], False)
            t = lax.dot_general(lhs, right_operand(blk, e), (((1,), (1,)), ((), ())), preferred_element_type=F32)
            for u in range(4):
                add_row(outs[u], r[u], pick(t, u, u >> 1, False))
        return carry

    lax.fori_loop(0, codes[LIST - 1] // UNROLL, some, 0)


def clear(ref):
    def zero(d, carry):
        ref[d] = jnp.zeros((8, 128), F32)
        return carry

    lax.fori_loop(0, ref.shape[0], zero, 0, unroll=8)


def set_rows(grow, value):
    rows = value.shape[0]
    grow[0 : rows // 8] = value.reshape(rows // 8, 8, 128)
    grow[rows // 8 :] = jnp.zeros((grow.shape[0] - rows // 8, 8, 128), F32)


def quarter():
    lane = lax.broadcasted_iota(jnp.int32, (8, 128), 1) // (128 // 4)
    return (lane - lax.axis_index("rows")) & 3


def send_partials(stage, index, meta, square, flag, out):
    part = quarter()
    lane = lax.broadcasted_iota(jnp.int32, (8, 128), 1)
    three = spread(square).astype(F32)
    sums = jnp.where(part == 1, three[0:1, :], jnp.where(part == 2, three[1:2, :], three[2:3, :]))
    raised = (part == 0) & (lane % PACKET == ROOM)
    for d in range(index.shape[0]):
        meta[d] = jnp.where(part != 0, sums, jnp.where(raised, flag, index[d]))
    tiles = PACKET // 8
    last = lax.broadcasted_iota(jnp.int32, (PACKET, 128), 0) == ROOM

    def put(d, carry):
        row = jnp.broadcast_to(meta[d >> 3, pl.ds(d & 7, 1), :], (PACKET, 128))
        rows = stage[pl.ds(d * tiles, tiles)].reshape(PACKET, 128)
        out[d] = jnp.where(last, row, rows).astype(BF16)
        return carry

    lax.fori_loop(0, out.shape[0], put, 0, unroll=4)


def rhs_of(labels, weight):
    return weight[...] * (2 * labels[...] - 1).astype(F32)


def place_entries(own, peers, cols, counts, entries, index):
    slots, rows = cols.shape
    first = lax.axis_index("feat") * (own * peers)
    lane0 = (lax.axis_index("rows") & 3) * PACKET
    owner_id = lax.broadcasted_iota(jnp.int32, (peers, rows), 0)
    down = lax.broadcasted_iota(jnp.int32, (rows, rows), 0)
    earlier = jnp.where(down < lax.broadcasted_iota(jnp.int32, (rows, rows), 1), 1.0, 0.0).astype(BF16)
    before = jnp.zeros((peers, 1), F32)
    meta = jnp.zeros((peers, rows), F32)
    for s in range(slots):
        c = cols[s : s + 1, :] - first
        owner = lax.shift_right_logical(c, own.bit_length() - 1)
        live = s < counts[...]
        hit = jnp.where((owner_id == owner) & live, 1.0, 0.0)
        rank = before + jnp.dot(hit.astype(BF16), earlier, preferred_element_type=F32)
        before = before + jnp.sum(hit, axis=1, keepdims=True)
        rank = jnp.sum(hit * rank, axis=0, keepdims=True).astype(jnp.int32)
        fits = live & (rank < ROOM)
        across = lax.broadcasted_iota(jnp.int32, (1, rows), 1)
        code = (across << 12) | ((across * slots + s) << 20)
        entries[s : s + 1, :] = code | jnp.where(fits, owner * PACKET + rank, peers * PACKET)
        entries[slots + s : slots + s + 1, :] = code | c
        entries[2 * slots + s : 2 * slots + s + 1, :] = jnp.where(live, 1, 0)
        lane = jnp.where(fits, rank + lane0, -1)
        known = ((c & (own - 1)) + 1).astype(F32)
        spot = jnp.where(down == lane, 1.0, 0.0).astype(BF16)
        meta = meta + lax.dot_general(
            (hit * known).astype(BF16), spot, (((1,), (1,)), ((), ())), preferred_element_type=F32
        )
    index[...] = meta.reshape(index.shape)
    return jnp.where(jnp.max(before, axis=0, keepdims=True) > ROOM, RAISED, 0.0)


def first_backward(
    own, col_hbm, cnt_hbm, labels_hbm, weight_hbm, blocks, out, held, forth, back, index,
    cols, counts, entries, labels, weight, wide, entry_tile, stage, meta, sems, small_sems,
):
    slots, rows = cols.shape
    each = held.shape[0] // COPIES
    per_step = 8 * slots // each

    def block_copy(i):
        at = pl.ds(i * each, each)
        return pltpu.make_async_copy(blocks.at[at], held.at[at], sems.at[i])

    pairs = ((col_hbm, cols), (cnt_hbm, counts), (labels_hbm, labels), (weight_hbm, weight))
    small = [pltpu.make_async_copy(src, dst, small_sems.at[i]) for i, (src, dst) in enumerate(pairs)]
    for copy in small:
        copy.start()
    for i in range(EARLY):
        block_copy(i).start()
    for copy in small:
        copy.wait()
    flag = place_entries(own, out.shape[0], cols, counts, entry_tile, index)
    to_scalars = pltpu.make_async_copy(entry_tile, entries, small_sems.at[len(pairs)])
    to_scalars.start(priority=1)
    for i in range(EARLY, COPIES):
        block_copy(i).start()
    resid = rhs_of(labels, weight)
    rowed = (weight[...] * resid).astype(BF16).astype(F32)
    odd = lax.broadcasted_iota(jnp.int32, rowed.shape, 0) & 1
    wide[:, 0:128] = jnp.where(odd == 0, rowed, 0.0)
    wide[:, 128:256] = jnp.where(odd == 1, rowed, 0.0)
    clear(stage)
    to_scalars.wait()

    def step(p, k):
        r0 = pl.multiple_of(p * 8, 8)
        for i in range(per_step):
            block_copy(p * per_step + i).wait()
        lhs = wide[pl.ds(r0, 8), :].astype(BF16)
        for pair in range(4):
            for h in range(slots // 2):
                e = [(r0 + 2 * pair + q) * slots + 2 * h + s for q in range(2) for s in range(2)]
                t = jnp.dot(lhs, right_operand(held, e), preferred_element_type=F32)
                for u in range(4):
                    m, slot = 2 * pair + u // 2, 2 * h + u % 2
                    r = r0 + m
                    code = entries[slot, r]
                    put_row(stage, code & 4095, pick(t, m, u % 2, False))
                    back[k] = code
                    forth[k] = entries[slots + slot, r]
                    k = k + entries[2 * slots + slot, r]
        return k

    live = lax.fori_loop(0, rows // 8, step, 0)
    for u in range(UNROLL):
        forth[live + u] = rows << 12
        back[live + u] = (rows << 12) | (out.shape[0] * PACKET)
    end = ((live + UNROLL - 1) // UNROLL) * UNROLL
    forth[LIST - 1] = end
    back[LIST - 1] = end
    send_partials(stage, index, meta, total_sum(resid * resid), flag, out)


def next_backward(codes, labels, weight, mine, other, scal, index, held, out, resid_out, scal_out, grow, stage, meta):
    rows = weight.shape[0]
    clear(stage)
    both = mine[rows:, :] + other[rows:, :]
    alpha = jnp.sqrt(gathered_sum(both[0:3, :]) + EPS)
    unit = rhs_of(labels, weight) / scal[0:1, 0:1]
    resid = weight[...] * ((mine[0:rows, :] + other[0:rows, :]) / alpha) - alpha * unit
    resid_out[...] = resid
    scal_out[...] = pair_tile(alpha, both[3:4, 0:1])
    set_rows(grow, weight[...] * resid)
    backward_list(codes, held, grow, stage)
    send_partials(stage, index, meta, total_sum(resid * resid), 0.0, out)


def pair_tile(a, b):
    row = lax.broadcasted_iota(jnp.int32, (8, 128), 0)
    return jnp.where(row == 0, jnp.broadcast_to(a, (8, 128)), jnp.broadcast_to(b, (8, 128)))


def reduced(own, recv):
    lane = lax.broadcasted_iota(jnp.int32, (1, 128), 1) // PACKET
    feature = (lax.broadcasted_iota(jnp.int32, (own, 128), 0) + 1).astype(F32)
    acc = jnp.zeros((own, 128), F32)
    sums = jnp.zeros((1, 128), F32)
    most = jnp.zeros((1, 128), F32)
    for g in range(recv.shape[0] // 4):
        known = jnp.zeros((1, 128), F32)
        for j in range(4):
            row = recv[4 * g + j, PACKET - 8 : PACKET, :].astype(F32)[7:8, :]
            known = known + jnp.where(lane == j, row, 0.0)
            sums = sums + jnp.where(lane == j, 0.0, row)
        most = jnp.maximum(most, known)
        chosen = jnp.where(feature == known, 1.0, 0.0).astype(BF16)
        acc = acc + jnp.dot(chosen, recv[4 * g : 4 * g + 4].reshape(128, 128), preferred_element_type=F32)
    first = lax.broadcasted_iota(jnp.int32, (1, 128), 1) % PACKET == 0
    total = jnp.sum(jnp.where(first, sums, 0.0), axis=1, keepdims=True)
    return acc, jnp.sqrt(total + EPS), jnp.max(most, axis=1, keepdims=True)


def send_step(own, out, step_vec, scale):
    data = (scale * step_vec).astype(BF16)
    tile = spread(total_sum(step_vec * step_vec))

    def put(d, carry):
        out[d, 0:own, :] = data
        out[d, own : own + META, :] = tile
        return carry

    lax.fori_loop(0, out.shape[0], put, 0, unroll=8)


def first_owner(own, recv, scale_hbm, out, step_out, beta_out, scale, sem):
    start = pl.multiple_of(lax.axis_index("rows") * own, own)
    copy = pltpu.make_async_copy(scale_hbm.at[pl.ds(start, own), :], scale, sem)
    copy.start()
    total, beta, most = reduced(own, recv)
    copy.wait()
    step_vec = scale[...] * total / beta
    step_out[...] = step_vec
    beta_out[...] = pair_tile(beta, jnp.where(most > own, 1.0, 0.0))
    send_step(own, out, step_vec, scale[...])


def next_owner(own, recv, step_in, alpha_in, scale_hbm, out, beta_out, scale, sem):
    start = pl.multiple_of(lax.axis_index("rows") * own, own)
    copy = pltpu.make_async_copy(scale_hbm.at[pl.ds(start, own), :], scale, sem)
    copy.start()
    total, beta, _ = reduced(own, recv)
    copy.wait()
    unit = step_in[...] / alpha_in[0:1, 0:1]
    step_vec = scale[...] * total / beta - beta * unit
    beta_out[...] = jnp.broadcast_to(beta, beta_out.shape)
    send_step(own, out, step_vec, scale[...])


def forward(own, codes, recv, scal, held, out, table, *outs):
    rows = out.shape[0] - META
    tiles = own // 8

    def fill(d, meta):
        table[pl.ds(d * tiles, tiles)] = recv[d, 0:own, :].astype(F32).reshape(tiles, 8, 128)
        return meta + recv[d, own : own + META, :].astype(F32)

    meta = lax.fori_loop(0, recv.shape[0], fill, jnp.zeros((META, 128), F32), unroll=2)
    row = lax.broadcasted_iota(jnp.int32, (META, 128), 0)
    out[rows:, :] = jnp.where(row == 3, scal[1:2, :], meta)
    for ref in outs:
        ref[...] = jnp.zeros_like(ref)
    forward_list(codes, held, table, outs)
    acc = outs[0][0 : rows // 8]
    for ref in outs[1:]:
        acc = acc + ref[0 : rows // 8]
    out[0:rows, :] = acc.reshape(rows, 128)


def last_rows(weight, mine, other, resid_in, beta_in, resid_out, alpha_out, out):
    rows = weight.shape[0]
    both = mine[rows:, :] + other[rows:, :]
    alpha = jnp.sqrt(gathered_sum(both[0:3, :]) + EPS)
    unit = resid_in[...] / beta_in[0:1, 0:1]
    resid = weight[...] * ((mine[0:rows, :] + other[0:rows, :]) / alpha) - alpha * unit
    resid_out[...] = resid
    alpha_out[...] = jnp.broadcast_to(alpha, alpha_out.shape)
    out[...] = jnp.broadcast_to(total_sum(resid * resid), out.shape)


def combine(own, recv0, recv1, scale, squares, beta0, alpha0, beta1, alpha1, out_hbm, flag, out, sems):
    b0, a0 = beta0[0:1, 0:1], alpha0[0:1, 0:1]
    b1, a1 = beta1[0:1, 0:1], alpha1[0:1, 0:1]
    b2 = jnp.sqrt(jnp.sum(squares[...], axis=0, keepdims=True)[:, 0:1] + EPS)
    rho1 = jnp.sqrt(a0 * a0 + b1 * b1)
    cos1, sin1 = a0 / rho1, b1 / rho1
    theta1, bar1 = sin1 * a1, -cos1 * a1
    phi1, phibar1 = cos1 * b0, sin1 * b0
    rho2 = jnp.sqrt(bar1 * bar1 + b2 * b2)
    phi2 = (bar1 / rho2) * phibar1
    second = phi2 / rho2
    first = phi1 / rho1 - second * (theta1 / rho1)
    first, second = first / a0, second / a1
    flag[0, 0] = jnp.max(alpha0[1:2, :])
    n = sems.shape[0]
    each = out.shape[0] // n

    def copy(i):
        at = pl.ds(pl.multiple_of(i * each, each), each)
        return pltpu.make_async_copy(out.at[at], out_hbm.at[at], sems.at[i])

    def put(i, carry):
        for j in range(each // own):
            d = i * (each // own) + j
            at = pl.ds(pl.multiple_of(d * own, own), own)
            mixed = first * recv0[d, 0:own, :].astype(F32) + second * recv1[d, 0:own, :].astype(F32)
            out[at, :] = mixed / scale[at, :]
        copy(i).start()
        return carry

    lax.fori_loop(0, n, put, 0)
    lax.fori_loop(0, n, lambda i, carry: (copy(i).wait(), carry)[1], 0)


def general(blocks, col_index, row_counts, labels, row_weight, feature_scale):
    feat_local, side = feature_scale.shape
    peers = lax.axis_size("rows")
    local_col = col_index.T - lax.axis_index("feat") * feat_local
    live = (lax.broadcasted_iota(jnp.int32, local_col.shape, 0) < row_counts.T).astype(F32)

    def over_rows(x):
        return jnp.sum(lax.all_to_all(jnp.broadcast_to(x, (peers, 8, 128)), "rows", 0, 0), axis=0)[0, 0]

    def over_feat(x):
        return x + lax.ppermute(x, "feat", [(0, 1), (1, 0)])

    def backward(resid):
        rowed = (row_weight * resid).astype(BF16)
        terms = jnp.einsum("rsij,ri->srj", blocks, rowed, preferred_element_type=F32) * live[:, :, None]
        partial = jax.ops.segment_sum(terms.reshape(-1, side), local_col.reshape(-1), num_segments=feat_local)
        owned = jnp.sum(lax.all_to_all(partial.reshape(peers, -1, side), "rows", 0, 0), axis=0)
        total = lax.all_to_all(jnp.broadcast_to(owned, (peers,) + owned.shape), "rows", 0, 0).reshape(feat_local, side)
        return total, jnp.sqrt(over_rows(jnp.sum(resid * resid)) + EPS)

    def norm(step_vec):
        return jnp.sqrt(over_feat(jnp.full((8, 128), jnp.sum(step_vec * step_vec)))[0, 0] + EPS)

    resid = row_weight * (2 * labels - 1).astype(F32)
    total, beta = backward(resid)
    step_vec = feature_scale * total / beta
    alpha = norm(step_vec)
    unit_feat = step_vec / alpha
    start = (resid, beta, alpha, unit_feat, beta, alpha, unit_feat, jnp.zeros_like(unit_feat))

    def iteration(_, state):
        resid, beta, alpha, unit_feat, phi_bar, rho_bar, search, result = state
        scaled = (feature_scale * unit_feat).astype(BF16)
        picked = jnp.take(scaled, local_col, axis=0)
        terms = jnp.einsum("rsij,srj->sri", blocks, picked, preferred_element_type=F32)
        resid = row_weight * over_feat(jnp.sum(terms * live[:, :, None], axis=0)) - alpha * (resid / beta)
        total, beta = backward(resid)
        step_vec = feature_scale * total / beta - beta * unit_feat
        alpha = norm(step_vec)
        unit_feat = step_vec / alpha
        rho = jnp.sqrt(rho_bar * rho_bar + beta * beta)
        cosine, sine = rho_bar / rho, beta / rho
        theta, rho_bar = sine * alpha, -cosine * alpha
        phi, phi_bar = cosine * phi_bar, sine * phi_bar
        result = result + phi / rho * search
        search = unit_feat - theta / rho * search
        return (resid, beta, alpha, unit_feat, phi_bar, rho_bar, search, result)

    state = lax.fori_loop(0, ITERS, iteration, start)
    return state[-1], state[0]


def body(blocks, col_index, row_counts, labels, row_weight, feature_scale):
    rows, slots, side, _ = blocks.shape
    feat_local = feature_scale.shape[0]
    peers = lax.axis_size("rows")
    own = feat_local // peers
    far = [pltpu.with_memory_space_constraint(x, pltpu.HBM) for x in (col_index.T, row_counts.T, labels, row_weight)]
    far_blocks = pltpu.with_memory_space_constraint(blocks.reshape(rows * slots, side, side), pltpu.HBM)
    smem = pl.BlockSpec(memory_space=pltpu.SMEM)
    vmem = pl.BlockSpec(memory_space=pltpu.VMEM)
    hbm = pl.BlockSpec(memory_space=pltpu.HBM)
    small = jax.ShapeDtypeStruct((8, 128), F32)
    rowvec = jax.ShapeDtypeStruct((rows, side), F32)
    packet = jax.ShapeDtypeStruct((peers, own + META, side), BF16)
    sparse = jax.ShapeDtypeStruct((peers, PACKET, side), BF16)
    part = jax.ShapeDtypeStruct((rows + META, side), F32)
    listed = jax.ShapeDtypeStruct((LIST,), jnp.int32)
    marked = jax.ShapeDtypeStruct((peers // 8, 8, side), F32)
    params = pltpu.CompilerParams(vmem_limit_bytes=20 << 20)
    table = pltpu.VMEM((feat_local // 8, 8, side), F32)
    stage = pltpu.VMEM((peers * PACKET // 8 + 1, 8, side), F32)
    mark = pltpu.VMEM(marked.shape, F32)
    row_table = pltpu.VMEM((rows // 8 + 1, 8, side), F32)
    scale_scratch = [pltpu.VMEM((own, side), F32), pltpu.SemaphoreType.DMA]

    def exchange(x):
        return lax.all_to_all(x, "rows", 0, 0)

    def swap(x):
        return lax.ppermute(x, "feat", [(0, 1), (1, 0)])

    def forward_part(recv, scal):
        return pl.pallas_call(
            functools.partial(forward, own),
            out_shape=part,
            in_specs=[smem, vmem, vmem, vmem],
            out_specs=vmem,
            scratch_shapes=[table] + [row_table] * TABLES,
            compiler_params=params,
            name="forward",
        )(forth, recv, scal, held)

    send, held, forth, back, index = pl.pallas_call(
        functools.partial(first_backward, own),
        out_shape=(
            sparse,
            pltpu.VMEM((rows * slots, side, side), BF16),
            listed,
            listed,
            marked,
        ),
        in_specs=[hbm] * 5,
        out_specs=(vmem, vmem, smem, smem, vmem),
        scratch_shapes=[
            pltpu.VMEM((slots, rows), jnp.int32),
            pltpu.VMEM((1, rows), jnp.int32),
            pltpu.SMEM((3 * slots, rows), jnp.int32),
            pltpu.VMEM((rows, side), jnp.int32),
            pltpu.VMEM((rows, side), F32),
            pltpu.VMEM((rows, 2 * side), F32),
            pltpu.VMEM((3 * slots, rows), jnp.int32),
            stage,
            mark,
            pltpu.SemaphoreType.DMA((COPIES,)),
            pltpu.SemaphoreType.DMA((5,)),
        ],
        compiler_params=params,
        name="backward0",
    )(*far, far_blocks)
    send, step0, beta0 = pl.pallas_call(
        functools.partial(first_owner, own),
        out_shape=(packet, jax.ShapeDtypeStruct((own, side), F32), small),
        in_specs=[vmem, hbm],
        out_specs=(vmem, vmem, vmem),
        scratch_shapes=scale_scratch,
        compiler_params=params,
        name="owner0",
    )(exchange(send), feature_scale)
    recv0 = exchange(send)
    mine = forward_part(recv0, beta0)
    send, resid1, alpha0 = pl.pallas_call(
        next_backward,
        out_shape=(sparse, rowvec, small),
        in_specs=[smem] + [vmem] * 7,
        out_specs=(vmem, vmem, vmem),
        scratch_shapes=[row_table, stage, mark],
        compiler_params=params,
        name="backward1",
    )(back, labels, row_weight, mine, swap(mine), beta0, index, held)
    send, beta1 = pl.pallas_call(
        functools.partial(next_owner, own),
        out_shape=(packet, small),
        in_specs=[vmem, vmem, vmem, hbm],
        out_specs=(vmem, vmem),
        scratch_shapes=scale_scratch,
        compiler_params=params,
        name="owner1",
    )(exchange(send), step0, alpha0, feature_scale)
    recv1 = exchange(send)
    mine = forward_part(recv1, beta0)
    resid2, alpha1, send = pl.pallas_call(
        last_rows,
        out_shape=(rowvec, small, jax.ShapeDtypeStruct((peers, side), F32)),
        in_specs=[vmem] * 5,
        out_specs=(vmem, vmem, vmem),
        compiler_params=params,
        name="last_rows",
    )(row_weight, mine, swap(mine), resid1, beta1)
    result, flag = pl.pallas_call(
        functools.partial(combine, own),
        out_shape=(jax.ShapeDtypeStruct((feat_local, side), F32), jax.ShapeDtypeStruct((1, 1), F32)),
        in_specs=[vmem] * 8,
        out_specs=(hbm, smem),
        scratch_shapes=[pltpu.VMEM((feat_local, side), F32), pltpu.SemaphoreType.DMA((4,))],
        compiler_params=params,
        name="combine",
    )(recv0, recv1, feature_scale, exchange(send), beta0, alpha0, beta1, alpha1)

    def fits(state):
        return state[0] > 0.0

    def again(state):
        args = (blocks, col_index, row_counts, labels, row_weight, feature_scale)
        return (jnp.zeros_like(state[0]),) + general(*lax.optimization_barrier((state[0],) + args)[1:])

    _, result, resid2 = lax.while_loop(fits, again, (flag.reshape(()), result, resid2))
    return (result, resid2)


def solution(mesh):
    return jax.shard_map(
        body,
        mesh=mesh,
        in_specs=(
            P("rows", "feat", None, None),
            P("rows", "feat"),
            P("rows", "feat"),
            P("rows", None),
            P("rows", None),
            P("feat", None),
        ),
        out_specs=(P("feat", None), P("rows", None)),
        check_vma=False,
    )
```

```python
import functools

import jax
import jax.numpy as jnp
from jax import lax
from jax.experimental import pallas as pl
from jax.experimental.pallas import tpu as pltpu
from jax.sharding import PartitionSpec as P

F32 = jnp.float32
BF16 = jnp.bfloat16
EPS = 1e-06
ITERS = 2
META = 8
UNROLL = 64
COPIES = 16
EARLY = 1
LIST = 640
TABLES = 4
PACKET = 32
ROOM = PACKET - 1
RAISED = 128.0


def spread(value):
    full = jnp.broadcast_to(value, (META, 128))
    high = full.astype(BF16).astype(F32)
    rest = full - high
    mid = rest.astype(BF16).astype(F32)
    low = (rest - mid).astype(BF16).astype(F32)
    row = lax.broadcasted_iota(jnp.int32, (META, 128), 0)
    tile = jnp.where(row == 0, high, jnp.where(row == 1, mid, jnp.where(row == 2, low, 0.0)))
    return tile.astype(BF16)


def total_sum(x):
    return jnp.sum(jnp.sum(x, axis=0, keepdims=True), axis=1, keepdims=True)


def gathered_sum(tile):
    return jnp.sum(tile, axis=0, keepdims=True)[:, 0:1]


def decode(code):
    return code & 4095, (code >> 12) & 255, code >> 20


def tile_row(ref, i):
    return jnp.broadcast_to(ref[i >> 3, pl.ds(i & 7, 1), :], (8, 128))


def left_operand(parts, split):
    row = lax.broadcasted_iota(jnp.int32, (8, 128), 0)
    place = row & 3 if split else row
    halves = []
    for a, b in parts:
        x = jnp.where(place == a[0], a[1], jnp.where(place == b[0], b[1], 0.0))
        if split:
            high = x.astype(BF16).astype(F32)
            x = jnp.where(row < 4, high, x - high)
        halves.append(x.astype(BF16))
    return jnp.concatenate(halves, axis=1)


def right_operand(blk, e):
    top = jnp.concatenate([blk[e[0]], blk[e[1]]], axis=1)
    low = jnp.concatenate([blk[e[2]], blk[e[3]]], axis=1)
    return jnp.concatenate([top, low], axis=0)


def pick(t, m, half, split):
    lanes = slice(half * 128, half * 128 + 128)
    return t[m : m + 1, lanes] + t[m + 4 : m + 5, lanes] if split else t[m : m + 1, lanes]


def put_row(ref, i, value):
    ref[i >> 3, pl.ds(i & 7, 1), :] = value


def add_row(ref, i, value):
    ref[i >> 3, pl.ds(i & 7, 1), :] += value


def backward_list(codes, blk, grow, stage):
    def some(i, carry):
        for q in range(UNROLL // 4):
            at = i * UNROLL + q * 4
            c, r, e = zip(*[decode(codes[at + u]) for u in range(4)])
            g = [tile_row(grow, r[u]) for u in range(4)]
            lhs = left_operand([((0, g[0]), (1, g[1])), ((2, g[2]), (3, g[3]))], True)
            t = jnp.dot(lhs, right_operand(blk, e), preferred_element_type=F32)
            for u in range(4):
                put_row(stage, c[u], pick(t, u, u & 1, True))
        return carry

    lax.fori_loop(0, codes[LIST - 1] // UNROLL, some, 0)


def forward_list(codes, blk, table, outs):
    def some(i, carry):
        for q in range(UNROLL // 4):
            at = i * UNROLL + q * 4
            c, r, e = zip(*[decode(codes[at + u]) for u in range(4)])
            v = [tile_row(table, c[u]) for u in range(4)]
            lhs = left_operand([((0, v[0]), (2, v[2])), ((1, v[1]), (3, v[3]))], False)
            t = lax.dot_general(lhs, right_operand(blk, e), (((1,), (1,)), ((), ())), preferred_element_type=F32)
            for u in range(4):
                add_row(outs[u], r[u], pick(t, u, u >> 1, False))
        return carry

    lax.fori_loop(0, codes[LIST - 1] // UNROLL, some, 0)


def clear(ref):
    def zero(d, carry):
        ref[d] = jnp.zeros((8, 128), F32)
        return carry

    lax.fori_loop(0, ref.shape[0], zero, 0, unroll=8)


def set_rows(grow, value):
    rows = value.shape[0]
    grow[0 : rows // 8] = value.reshape(rows // 8, 8, 128)
    grow[rows // 8 :] = jnp.zeros((grow.shape[0] - rows // 8, 8, 128), F32)


def quarter():
    lane = lax.broadcasted_iota(jnp.int32, (8, 128), 1) // (128 // 4)
    return (lane - lax.axis_index("rows")) & 3


def send_partials(stage, index, meta, square, flag, out):
    part = quarter()
    lane = lax.broadcasted_iota(jnp.int32, (8, 128), 1)
    three = spread(square).astype(F32)
    sums = jnp.where(part == 1, three[0:1, :], jnp.where(part == 2, three[1:2, :], three[2:3, :]))
    raised = (part == 0) & (lane % PACKET == ROOM)
    for d in range(index.shape[0]):
        meta[d] = jnp.where(part != 0, sums, jnp.where(raised, flag, index[d]))
    tiles = PACKET // 8
    last = lax.broadcasted_iota(jnp.int32, (PACKET, 128), 0) == ROOM

    def put(d, carry):
        row = jnp.broadcast_to(meta[d >> 3, pl.ds(d & 7, 1), :], (PACKET, 128))
        rows = stage[pl.ds(d * tiles, tiles)].reshape(PACKET, 128)
        out[d] = jnp.where(last, row, rows).astype(BF16)
        return carry

    lax.fori_loop(0, out.shape[0], put, 0, unroll=4)


def rhs_of(labels, weight):
    return weight[...] * (2 * labels[...] - 1).astype(F32)


def place_entries(own, peers, cols, counts, entries, index):
    slots, rows = cols.shape
    first = lax.axis_index("feat") * (own * peers)
    lane0 = (lax.axis_index("rows") & 3) * PACKET
    owner_id = lax.broadcasted_iota(jnp.int32, (peers, rows), 0)
    down = lax.broadcasted_iota(jnp.int32, (rows, rows), 0)
    earlier = jnp.where(down < lax.broadcasted_iota(jnp.int32, (rows, rows), 1), 1.0, 0.0).astype(BF16)
    before = jnp.zeros((peers, 1), F32)
    meta = jnp.zeros((peers, rows), F32)
    for s in range(slots):
        c = cols[s : s + 1, :] - first
        owner = lax.shift_right_logical(c, own.bit_length() - 1)
        live = s < counts[...]
        hit = jnp.where((owner_id == owner) & live, 1.0, 0.0)
        rank = before + jnp.dot(hit.astype(BF16), earlier, preferred_element_type=F32)
        before = before + jnp.sum(hit, axis=1, keepdims=True)
        rank = jnp.sum(hit * rank, axis=0, keepdims=True).astype(jnp.int32)
        fits = live & (rank < ROOM)
        across = lax.broadcasted_iota(jnp.int32, (1, rows), 1)
        code = (across << 12) | ((across * slots + s) << 20)
        entries[s : s + 1, :] = code | jnp.where(fits, owner * PACKET + rank, peers * PACKET)
        entries[slots + s : slots + s + 1, :] = code | c
        entries[2 * slots + s : 2 * slots + s + 1, :] = jnp.where(live, 1, 0)
        lane = jnp.where(fits, rank + lane0, -1)
        known = ((c & (own - 1)) + 1).astype(F32)
        spot = jnp.where(down == lane, 1.0, 0.0).astype(BF16)
        meta = meta + lax.dot_general(
            (hit * known).astype(BF16), spot, (((1,), (1,)), ((), ())), preferred_element_type=F32
        )
    index[...] = meta.reshape(index.shape)
    return jnp.where(jnp.max(before, axis=0, keepdims=True) > ROOM, RAISED, 0.0)


def first_backward(
    own, col_hbm, cnt_hbm, labels_hbm, weight_hbm, blocks, out, held, forth, back, index,
    cols, counts, entries, labels, weight, wide, entry_tile, stage, meta, sems, small_sems,
):
    slots, rows = cols.shape
    each = held.shape[0] // COPIES
    per_step = 8 * slots // each

    def block_copy(i):
        at = pl.ds(i * each, each)
        return pltpu.make_async_copy(blocks.at[at], held.at[at], sems.at[i])

    pairs = ((col_hbm, cols), (cnt_hbm, counts), (labels_hbm, labels), (weight_hbm, weight))
    small = [pltpu.make_async_copy(src, dst, small_sems.at[i]) for i, (src, dst) in enumerate(pairs)]
    for copy in small:
        copy.start()
    for i in range(EARLY):
        block_copy(i).start()
    for copy in small[:2]:
        copy.wait()
    flag = place_entries(own, out.shape[0], cols, counts, entry_tile, index)
    to_scalars = pltpu.make_async_copy(entry_tile, entries, small_sems.at[len(pairs)])
    to_scalars.start(priority=1)
    for i in range(EARLY, COPIES):
        block_copy(i).start()
    for copy in small[2:]:
        copy.wait()
    resid = rhs_of(labels, weight)
    rowed = (weight[...] * resid).astype(BF16).astype(F32)
    odd = lax.broadcasted_iota(jnp.int32, rowed.shape, 0) & 1
    wide[:, 0:128] = jnp.where(odd == 0, rowed, 0.0)
    wide[:, 128:256] = jnp.where(odd == 1, rowed, 0.0)
    clear(stage)
    to_scalars.wait()

    def step(p, k):
        r0 = pl.multiple_of(p * 8, 8)
        for i in range(per_step):
            block_copy(p * per_step + i).wait()
        lhs = wide[pl.ds(r0, 8), :].astype(BF16)
        for pair in range(4):
            for h in range(slots // 2):
                e = [(r0 + 2 * pair + q) * slots + 2 * h + s for q in range(2) for s in range(2)]
                t = jnp.dot(lhs, right_operand(held, e), preferred_element_type=F32)
                for u in range(4):
                    m, slot = 2 * pair + u // 2, 2 * h + u % 2
                    r = r0 + m
                    code = entries[slot, r]
                    put_row(stage, code & 4095, pick(t, m, u % 2, False))
                    back[k] = code
                    forth[k] = entries[slots + slot, r]
                    k = k + entries[2 * slots + slot, r]
        return k

    live = lax.fori_loop(0, rows // 8, step, 0)
    for u in range(UNROLL):
        forth[live + u] = rows << 12
        back[live + u] = (rows << 12) | (out.shape[0] * PACKET)
    end = ((live + UNROLL - 1) // UNROLL) * UNROLL
    forth[LIST - 1] = end
    back[LIST - 1] = end
    send_partials(stage, index, meta, total_sum(resid * resid), flag, out)


def next_backward(codes, labels, weight, mine, other, scal, index, held, out, resid_out, scal_out, grow, stage, meta):
    rows = weight.shape[0]
    clear(stage)
    both = mine[rows:, :] + other[rows:, :]
    alpha = jnp.sqrt(gathered_sum(both[0:3, :]) + EPS)
    unit = rhs_of(labels, weight) / scal[0:1, 0:1]
    resid = weight[...] * ((mine[0:rows, :] + other[0:rows, :]) / alpha) - alpha * unit
    resid_out[...] = resid
    scal_out[...] = pair_tile(alpha, both[3:4, 0:1])
    set_rows(grow, weight[...] * resid)
    backward_list(codes, held, grow, stage)
    send_partials(stage, index, meta, total_sum(resid * resid), 0.0, out)


def pair_tile(a, b):
    row = lax.broadcasted_iota(jnp.int32, (8, 128), 0)
    return jnp.where(row == 0, jnp.broadcast_to(a, (8, 128)), jnp.broadcast_to(b, (8, 128)))


def reduced(own, recv):
    lane = lax.broadcasted_iota(jnp.int32, (1, 128), 1) // PACKET
    feature = (lax.broadcasted_iota(jnp.int32, (own, 128), 0) + 1).astype(F32)
    acc = jnp.zeros((own, 128), F32)
    sums = jnp.zeros((1, 128), F32)
    most = jnp.zeros((1, 128), F32)
    for g in range(recv.shape[0] // 4):
        known = jnp.zeros((1, 128), F32)
        for j in range(4):
            row = recv[4 * g + j, PACKET - 8 : PACKET, :].astype(F32)[7:8, :]
            known = known + jnp.where(lane == j, row, 0.0)
            sums = sums + jnp.where(lane == j, 0.0, row)
        most = jnp.maximum(most, known)
        chosen = jnp.where(feature == known, 1.0, 0.0).astype(BF16)
        acc = acc + jnp.dot(chosen, recv[4 * g : 4 * g + 4].reshape(128, 128), preferred_element_type=F32)
    first = lax.broadcasted_iota(jnp.int32, (1, 128), 1) % PACKET == 0
    total = jnp.sum(jnp.where(first, sums, 0.0), axis=1, keepdims=True)
    return acc, jnp.sqrt(total + EPS), jnp.max(most, axis=1, keepdims=True)


def send_step(own, out, step_vec, scale):
    data = (scale * step_vec).astype(BF16)
    tile = spread(total_sum(step_vec * step_vec))

    def put(d, carry):
        out[d, 0:own, :] = data
        out[d, own : own + META, :] = tile
        return carry

    lax.fori_loop(0, out.shape[0], put, 0, unroll=8)


def first_owner(own, recv, scale_hbm, out, step_out, beta_out, scale, sem):
    start = pl.multiple_of(lax.axis_index("rows") * own, own)
    copy = pltpu.make_async_copy(scale_hbm.at[pl.ds(start, own), :], scale, sem)
    copy.start()
    total, beta, most = reduced(own, recv)
    copy.wait()
    step_vec = scale[...] * total / beta
    step_out[...] = step_vec
    beta_out[...] = pair_tile(beta, jnp.where(most > own, 1.0, 0.0))
    send_step(own, out, step_vec, scale[...])


def next_owner(own, recv, step_in, alpha_in, scale_hbm, out, beta_out, scale, sem):
    start = pl.multiple_of(lax.axis_index("rows") * own, own)
    copy = pltpu.make_async_copy(scale_hbm.at[pl.ds(start, own), :], scale, sem)
    copy.start()
    total, beta, _ = reduced(own, recv)
    copy.wait()
    unit = step_in[...] / alpha_in[0:1, 0:1]
    step_vec = scale[...] * total / beta - beta * unit
    beta_out[...] = jnp.broadcast_to(beta, beta_out.shape)
    send_step(own, out, step_vec, scale[...])


def forward(own, codes, recv, scal, held, out, table, *outs):
    rows = out.shape[0] - META
    tiles = own // 8

    def fill(d, meta):
        table[pl.ds(d * tiles, tiles)] = recv[d, 0:own, :].astype(F32).reshape(tiles, 8, 128)
        return meta + recv[d, own : own + META, :].astype(F32)

    meta = lax.fori_loop(0, recv.shape[0], fill, jnp.zeros((META, 128), F32), unroll=8)
    row = lax.broadcasted_iota(jnp.int32, (META, 128), 0)
    out[rows:, :] = jnp.where(row == 3, scal[1:2, :], meta)
    for ref in outs:
        ref[...] = jnp.zeros_like(ref)
    forward_list(codes, held, table, outs)
    acc = outs[0][0 : rows // 8]
    for ref in outs[1:]:
        acc = acc + ref[0 : rows // 8]
    out[0:rows, :] = acc.reshape(rows, 128)


def last_rows(weight, mine, other, resid_in, beta_in, resid_out, alpha_out, out):
    rows = weight.shape[0]
    both = mine[rows:, :] + other[rows:, :]
    alpha = jnp.sqrt(gathered_sum(both[0:3, :]) + EPS)
    unit = resid_in[...] / beta_in[0:1, 0:1]
    resid = weight[...] * ((mine[0:rows, :] + other[0:rows, :]) / alpha) - alpha * unit
    resid_out[...] = resid
    alpha_out[...] = jnp.broadcast_to(alpha, alpha_out.shape)
    out[...] = jnp.broadcast_to(total_sum(resid * resid), out.shape)


def combine(own, recv0, recv1, scale, squares, beta0, alpha0, beta1, alpha1, out_hbm, flag, out, sems):
    b0, a0 = beta0[0:1, 0:1], alpha0[0:1, 0:1]
    b1, a1 = beta1[0:1, 0:1], alpha1[0:1, 0:1]
    b2 = jnp.sqrt(jnp.sum(squares[...], axis=0, keepdims=True)[:, 0:1] + EPS)
    rho1 = jnp.sqrt(a0 * a0 + b1 * b1)
    cos1, sin1 = a0 / rho1, b1 / rho1
    theta1, bar1 = sin1 * a1, -cos1 * a1
    phi1, phibar1 = cos1 * b0, sin1 * b0
    rho2 = jnp.sqrt(bar1 * bar1 + b2 * b2)
    phi2 = (bar1 / rho2) * phibar1
    second = phi2 / rho2
    first = phi1 / rho1 - second * (theta1 / rho1)
    first, second = first / a0, second / a1
    flag[0, 0] = jnp.max(alpha0[1:2, :])
    n = sems.shape[0]
    each = out.shape[0] // n

    def copy(i):
        at = pl.ds(pl.multiple_of(i * each, each), each)
        return pltpu.make_async_copy(out.at[at], out_hbm.at[at], sems.at[i])

    def put(i, carry):
        for j in range(each // own):
            d = i * (each // own) + j
            at = pl.ds(pl.multiple_of(d * own, own), own)
            mixed = first * recv0[d, 0:own, :].astype(F32) + second * recv1[d, 0:own, :].astype(F32)
            out[at, :] = mixed / scale[at, :]
        copy(i).start()
        return carry

    lax.fori_loop(0, n, put, 0)
    lax.fori_loop(0, n, lambda i, carry: (copy(i).wait(), carry)[1], 0)


def general(blocks, col_index, row_counts, labels, row_weight, feature_scale):
    feat_local, side = feature_scale.shape
    peers = lax.axis_size("rows")
    local_col = col_index.T - lax.axis_index("feat") * feat_local
    live = (lax.broadcasted_iota(jnp.int32, local_col.shape, 0) < row_counts.T).astype(F32)

    def over_rows(x):
        return jnp.sum(lax.all_to_all(jnp.broadcast_to(x, (peers, 8, 128)), "rows", 0, 0), axis=0)[0, 0]

    def over_feat(x):
        return x + lax.ppermute(x, "feat", [(0, 1), (1, 0)])

    def backward(resid):
        rowed = (row_weight * resid).astype(BF16)
        terms = jnp.einsum("rsij,ri->srj", blocks, rowed, preferred_element_type=F32) * live[:, :, None]
        partial = jax.ops.segment_sum(terms.reshape(-1, side), local_col.reshape(-1), num_segments=feat_local)
        owned = jnp.sum(lax.all_to_all(partial.reshape(peers, -1, side), "rows", 0, 0), axis=0)
        total = lax.all_to_all(jnp.broadcast_to(owned, (peers,) + owned.shape), "rows", 0, 0).reshape(feat_local, side)
        return total, jnp.sqrt(over_rows(jnp.sum(resid * resid)) + EPS)

    def norm(step_vec):
        return jnp.sqrt(over_feat(jnp.full((8, 128), jnp.sum(step_vec * step_vec)))[0, 0] + EPS)

    resid = row_weight * (2 * labels - 1).astype(F32)
    total, beta = backward(resid)
    step_vec = feature_scale * total / beta
    alpha = norm(step_vec)
    unit_feat = step_vec / alpha
    start = (resid, beta, alpha, unit_feat, beta, alpha, unit_feat, jnp.zeros_like(unit_feat))

    def iteration(_, state):
        resid, beta, alpha, unit_feat, phi_bar, rho_bar, search, result = state
        scaled = (feature_scale * unit_feat).astype(BF16)
        picked = jnp.take(scaled, local_col, axis=0)
        terms = jnp.einsum("rsij,srj->sri", blocks, picked, preferred_element_type=F32)
        resid = row_weight * over_feat(jnp.sum(terms * live[:, :, None], axis=0)) - alpha * (resid / beta)
        total, beta = backward(resid)
        step_vec = feature_scale * total / beta - beta * unit_feat
        alpha = norm(step_vec)
        unit_feat = step_vec / alpha
        rho = jnp.sqrt(rho_bar * rho_bar + beta * beta)
        cosine, sine = rho_bar / rho, beta / rho
        theta, rho_bar = sine * alpha, -cosine * alpha
        phi, phi_bar = cosine * phi_bar, sine * phi_bar
        result = result + phi / rho * search
        search = unit_feat - theta / rho * search
        return (resid, beta, alpha, unit_feat, phi_bar, rho_bar, search, result)

    state = lax.fori_loop(0, ITERS, iteration, start)
    return state[-1], state[0]


def body(blocks, col_index, row_counts, labels, row_weight, feature_scale):
    rows, slots, side, _ = blocks.shape
    feat_local = feature_scale.shape[0]
    peers = lax.axis_size("rows")
    own = feat_local // peers
    far = [pltpu.with_memory_space_constraint(x, pltpu.HBM) for x in (col_index.T, row_counts.T, labels, row_weight)]
    far_blocks = pltpu.with_memory_space_constraint(blocks.reshape(rows * slots, side, side), pltpu.HBM)
    smem = pl.BlockSpec(memory_space=pltpu.SMEM)
    vmem = pl.BlockSpec(memory_space=pltpu.VMEM)
    hbm = pl.BlockSpec(memory_space=pltpu.HBM)
    small = jax.ShapeDtypeStruct((8, 128), F32)
    rowvec = jax.ShapeDtypeStruct((rows, side), F32)
    packet = jax.ShapeDtypeStruct((peers, own + META, side), BF16)
    sparse = jax.ShapeDtypeStruct((peers, PACKET, side), BF16)
    part = jax.ShapeDtypeStruct((rows + META, side), F32)
    listed = jax.ShapeDtypeStruct((LIST,), jnp.int32)
    marked = jax.ShapeDtypeStruct((peers // 8, 8, side), F32)
    params = pltpu.CompilerParams(vmem_limit_bytes=20 << 20)
    table = pltpu.VMEM((feat_local // 8, 8, side), F32)
    stage = pltpu.VMEM((peers * PACKET // 8 + 1, 8, side), F32)
    mark = pltpu.VMEM(marked.shape, F32)
    row_table = pltpu.VMEM((rows // 8 + 1, 8, side), F32)
    scale_scratch = [pltpu.VMEM((own, side), F32), pltpu.SemaphoreType.DMA]

    def exchange(x):
        return lax.all_to_all(x, "rows", 0, 0)

    def swap(x):
        return lax.ppermute(x, "feat", [(0, 1), (1, 0)])

    def forward_part(recv, scal):
        return pl.pallas_call(
            functools.partial(forward, own),
            out_shape=part,
            in_specs=[smem, vmem, vmem, vmem],
            out_specs=vmem,
            scratch_shapes=[table] + [row_table] * TABLES,
            compiler_params=params,
            name="forward",
        )(forth, recv, scal, held)

    send, held, forth, back, index = pl.pallas_call(
        functools.partial(first_backward, own),
        out_shape=(
            sparse,
            pltpu.VMEM((rows * slots, side, side), BF16),
            listed,
            listed,
            marked,
        ),
        in_specs=[hbm] * 5,
        out_specs=(vmem, vmem, smem, smem, vmem),
        scratch_shapes=[
            pltpu.VMEM((slots, rows), jnp.int32),
            pltpu.VMEM((1, rows), jnp.int32),
            pltpu.SMEM((3 * slots, rows), jnp.int32),
            pltpu.VMEM((rows, side), jnp.int32),
            pltpu.VMEM((rows, side), F32),
            pltpu.VMEM((rows, 2 * side), F32),
            pltpu.VMEM((3 * slots, rows), jnp.int32),
            stage,
            mark,
            pltpu.SemaphoreType.DMA((COPIES,)),
            pltpu.SemaphoreType.DMA((5,)),
        ],
        compiler_params=params,
        name="backward0",
    )(*far, far_blocks)
    send, step0, beta0 = pl.pallas_call(
        functools.partial(first_owner, own),
        out_shape=(packet, jax.ShapeDtypeStruct((own, side), F32), small),
        in_specs=[vmem, hbm],
        out_specs=(vmem, vmem, vmem),
        scratch_shapes=scale_scratch,
        compiler_params=params,
        name="owner0",
    )(exchange(send), feature_scale)
    recv0 = exchange(send)
    mine = forward_part(recv0, beta0)
    send, resid1, alpha0 = pl.pallas_call(
        next_backward,
        out_shape=(sparse, rowvec, small),
        in_specs=[smem] + [vmem] * 7,
        out_specs=(vmem, vmem, vmem),
        scratch_shapes=[row_table, stage, mark],
        compiler_params=params,
        name="backward1",
    )(back, labels, row_weight, mine, swap(mine), beta0, index, held)
    send, beta1 = pl.pallas_call(
        functools.partial(next_owner, own),
        out_shape=(packet, small),
        in_specs=[vmem, vmem, vmem, hbm],
        out_specs=(vmem, vmem),
        scratch_shapes=scale_scratch,
        compiler_params=params,
        name="owner1",
    )(exchange(send), step0, alpha0, feature_scale)
    recv1 = exchange(send)
    mine = forward_part(recv1, beta0)
    resid2, alpha1, send = pl.pallas_call(
        last_rows,
        out_shape=(rowvec, small, jax.ShapeDtypeStruct((peers, side), F32)),
        in_specs=[vmem] * 5,
        out_specs=(vmem, vmem, vmem),
        compiler_params=params,
        name="last_rows",
    )(row_weight, mine, swap(mine), resid1, beta1)
    result, flag = pl.pallas_call(
        functools.partial(combine, own),
        out_shape=(jax.ShapeDtypeStruct((feat_local, side), F32), jax.ShapeDtypeStruct((1, 1), F32)),
        in_specs=[vmem] * 8,
        out_specs=(hbm, smem),
        scratch_shapes=[pltpu.VMEM((feat_local, side), F32), pltpu.SemaphoreType.DMA((4,))],
        compiler_params=params,
        name="combine",
    )(recv0, recv1, feature_scale, exchange(send), beta0, alpha0, beta1, alpha1)

    def fits(state):
        return state[0] > 0.0

    def again(state):
        args = (blocks, col_index, row_counts, labels, row_weight, feature_scale)
        return (jnp.zeros_like(state[0]),) + general(*lax.optimization_barrier((state[0],) + args)[1:])

    _, result, resid2 = lax.while_loop(fits, again, (flag.reshape(()), result, resid2))
    return (result, resid2)


def solution(mesh):
    return jax.shard_map(
        body,
        mesh=mesh,
        in_specs=(
            P("rows", "feat", None, None),
            P("rows", "feat"),
            P("rows", "feat"),
            P("rows", None),
            P("rows", None),
            P("feat", None),
        ),
        out_specs=(P("feat", None), P("rows", None)),
        check_vma=False,
    )
```

```python
import functools

import jax
import jax.numpy as jnp
from jax import lax
from jax.experimental import pallas as pl
from jax.experimental.pallas import tpu as pltpu
from jax.sharding import PartitionSpec as P

F32 = jnp.float32
BF16 = jnp.bfloat16
EPS = 1e-06
ITERS = 2
META = 8
UNROLL = 72
COPIES = 16
EARLY = 1
LIST = 640
TABLES = 4
PACKET = 32
ROOM = PACKET - 1
RAISED = 128.0


def spread(value):
    full = jnp.broadcast_to(value, (META, 128))
    high = full.astype(BF16).astype(F32)
    rest = full - high
    mid = rest.astype(BF16).astype(F32)
    low = (rest - mid).astype(BF16).astype(F32)
    row = lax.broadcasted_iota(jnp.int32, (META, 128), 0)
    tile = jnp.where(row == 0, high, jnp.where(row == 1, mid, jnp.where(row == 2, low, 0.0)))
    return tile.astype(BF16)


def total_sum(x):
    return jnp.sum(jnp.sum(x, axis=0, keepdims=True), axis=1, keepdims=True)


def gathered_sum(tile):
    return jnp.sum(tile, axis=0, keepdims=True)[:, 0:1]


def decode(code):
    return code & 4095, (code >> 12) & 255, code >> 20


def tile_row(ref, i):
    return jnp.broadcast_to(ref[i >> 3, pl.ds(i & 7, 1), :], (8, 128))


def left_operand(parts, split):
    row = lax.broadcasted_iota(jnp.int32, (8, 128), 0)
    place = row & 3 if split else row
    halves = []
    for a, b in parts:
        x = jnp.where(place == a[0], a[1], jnp.where(place == b[0], b[1], 0.0))
        if split:
            high = x.astype(BF16).astype(F32)
            x = jnp.where(row < 4, high, x - high)
        halves.append(x.astype(BF16))
    return jnp.concatenate(halves, axis=1)


def right_operand(blk, e):
    top = jnp.concatenate([blk[e[0]], blk[e[1]]], axis=1)
    low = jnp.concatenate([blk[e[2]], blk[e[3]]], axis=1)
    return jnp.concatenate([top, low], axis=0)


def pick(t, m, half, split):
    lanes = slice(half * 128, half * 128 + 128)
    return t[m : m + 1, lanes] + t[m + 4 : m + 5, lanes] if split else t[m : m + 1, lanes]


def put_row(ref, i, value):
    ref[i >> 3, pl.ds(i & 7, 1), :] = value


def add_row(ref, i, value):
    ref[i >> 3, pl.ds(i & 7, 1), :] += value


def backward_list(codes, blk, grow, stage):
    def some(i, carry):
        for q in range(UNROLL // 4):
            at = i * UNROLL + q * 4
            c, r, e = zip(*[decode(codes[at + u]) for u in range(4)])
            g = [tile_row(grow, r[u]) for u in range(4)]
            lhs = left_operand([((0, g[0]), (1, g[1])), ((2, g[2]), (3, g[3]))], True)
            t = jnp.dot(lhs, right_operand(blk, e), preferred_element_type=F32)
            for u in range(4):
                put_row(stage, c[u], pick(t, u, u & 1, True))
        return carry

    lax.fori_loop(0, codes[LIST - 1] // UNROLL, some, 0)


def forward_list(codes, blk, table, outs):
    def some(i, carry):
        for q in range(UNROLL // 4):
            at = i * UNROLL + q * 4
            c, r, e = zip(*[decode(codes[at + u]) for u in range(4)])
            v = [tile_row(table, c[u]) for u in range(4)]
            lhs = left_operand([((0, v[0]), (2, v[2])), ((1, v[1]), (3, v[3]))], False)
            t = lax.dot_general(lhs, right_operand(blk, e), (((1,), (1,)), ((), ())), preferred_element_type=F32)
            for u in range(4):
                add_row(outs[u], r[u], pick(t, u, u >> 1, False))
        return carry

    lax.fori_loop(0, codes[LIST - 1] // UNROLL, some, 0)


def clear(ref):
    def zero(d, carry):
        ref[d] = jnp.zeros((8, 128), F32)
        return carry

    lax.fori_loop(0, ref.shape[0], zero, 0, unroll=8)


def set_rows(grow, value):
    rows = value.shape[0]
    grow[0 : rows // 8] = value.reshape(rows // 8, 8, 128)
    grow[rows // 8 :] = jnp.zeros((grow.shape[0] - rows // 8, 8, 128), F32)


def quarter():
    lane = lax.broadcasted_iota(jnp.int32, (8, 128), 1) // (128 // 4)
    return (lane - lax.axis_index("rows")) & 3


def send_partials(stage, index, meta, square, flag, out):
    part = quarter()
    lane = lax.broadcasted_iota(jnp.int32, (8, 128), 1)
    three = spread(square).astype(F32)
    sums = jnp.where(part == 1, three[0:1, :], jnp.where(part == 2, three[1:2, :], three[2:3, :]))
    raised = (part == 0) & (lane % PACKET == ROOM)
    for d in range(index.shape[0]):
        meta[d] = jnp.where(part != 0, sums, jnp.where(raised, flag, index[d]))
    tiles = PACKET // 8
    last = lax.broadcasted_iota(jnp.int32, (PACKET, 128), 0) == ROOM

    def put(d, carry):
        row = jnp.broadcast_to(meta[d >> 3, pl.ds(d & 7, 1), :], (PACKET, 128))
        rows = stage[pl.ds(d * tiles, tiles)].reshape(PACKET, 128)
        out[d] = jnp.where(last, row, rows).astype(BF16)
        return carry

    lax.fori_loop(0, out.shape[0], put, 0, unroll=4)


def rhs_of(labels, weight):
    return weight[...] * (2 * labels[...] - 1).astype(F32)


def place_entries(own, peers, cols, counts, entries, index):
    slots, rows = cols.shape
    first = lax.axis_index("feat") * (own * peers)
    lane0 = (lax.axis_index("rows") & 3) * PACKET
    owner_id = lax.broadcasted_iota(jnp.int32, (peers, rows), 0)
    down = lax.broadcasted_iota(jnp.int32, (rows, rows), 0)
    earlier = jnp.where(down < lax.broadcasted_iota(jnp.int32, (rows, rows), 1), 1.0, 0.0).astype(BF16)
    before = jnp.zeros((peers, 1), F32)
    meta = jnp.zeros((peers, rows), F32)
    for s in range(slots):
        c = cols[s : s + 1, :] - first
        owner = lax.shift_right_logical(c, own.bit_length() - 1)
        live = s < counts[...]
        hit = jnp.where((owner_id == owner) & live, 1.0, 0.0)
        rank = before + jnp.dot(hit.astype(BF16), earlier, preferred_element_type=F32)
        before = before + jnp.sum(hit, axis=1, keepdims=True)
        rank = jnp.sum(hit * rank, axis=0, keepdims=True).astype(jnp.int32)
        fits = live & (rank < ROOM)
        across = lax.broadcasted_iota(jnp.int32, (1, rows), 1)
        code = (across << 12) | ((across * slots + s) << 20)
        entries[s : s + 1, :] = code | jnp.where(fits, owner * PACKET + rank, peers * PACKET)
        entries[slots + s : slots + s + 1, :] = code | c
        entries[2 * slots + s : 2 * slots + s + 1, :] = jnp.where(live, 1, 0)
        lane = jnp.where(fits, rank + lane0, -1)
        known = ((c & (own - 1)) + 1).astype(F32)
        spot = jnp.where(down == lane, 1.0, 0.0).astype(BF16)
        meta = meta + lax.dot_general(
            (hit * known).astype(BF16), spot, (((1,), (1,)), ((), ())), preferred_element_type=F32
        )
    index[...] = meta.reshape(index.shape)
    return jnp.where(jnp.max(before, axis=0, keepdims=True) > ROOM, RAISED, 0.0)


def first_backward(
    own, col_hbm, cnt_hbm, labels_hbm, weight_hbm, blocks, out, held, forth, back, index,
    cols, counts, entries, labels, weight, wide, entry_tile, stage, meta, sems, small_sems,
):
    slots, rows = cols.shape
    each = held.shape[0] // COPIES
    per_step = 8 * slots // each

    def block_copy(i):
        at = pl.ds(i * each, each)
        return pltpu.make_async_copy(blocks.at[at], held.at[at], sems.at[i])

    pairs = ((col_hbm, cols), (cnt_hbm, counts), (labels_hbm, labels), (weight_hbm, weight))
    small = [pltpu.make_async_copy(src, dst, small_sems.at[i]) for i, (src, dst) in enumerate(pairs)]
    for copy in small:
        copy.start()
    for i in range(EARLY):
        block_copy(i).start()
    for copy in small[:2]:
        copy.wait()
    flag = place_entries(own, out.shape[0], cols, counts, entry_tile, index)
    to_scalars = pltpu.make_async_copy(entry_tile, entries, small_sems.at[len(pairs)])
    to_scalars.start(priority=1)
    for i in range(EARLY, COPIES):
        block_copy(i).start()
    for copy in small[2:]:
        copy.wait()
    resid = rhs_of(labels, weight)
    rowed = (weight[...] * resid).astype(BF16).astype(F32)
    odd = lax.broadcasted_iota(jnp.int32, rowed.shape, 0) & 1
    wide[:, 0:128] = jnp.where(odd == 0, rowed, 0.0)
    wide[:, 128:256] = jnp.where(odd == 1, rowed, 0.0)
    clear(stage)
    to_scalars.wait()

    def step(p, k):
        r0 = pl.multiple_of(p * 8, 8)
        for i in range(per_step):
            block_copy(p * per_step + i).wait()
        lhs = wide[pl.ds(r0, 8), :].astype(BF16)
        for pair in range(4):
            for h in range(slots // 2):
                e = [(r0 + 2 * pair + q) * slots + 2 * h + s for q in range(2) for s in range(2)]
                t = jnp.dot(lhs, right_operand(held, e), preferred_element_type=F32)
                for u in range(4):
                    m, slot = 2 * pair + u // 2, 2 * h + u % 2
                    r = r0 + m
                    code = entries[slot, r]
                    put_row(stage, code & 4095, pick(t, m, u % 2, False))
                    back[k] = code
                    forth[k] = entries[slots + slot, r]
                    k = k + entries[2 * slots + slot, r]
        return k

    live = lax.fori_loop(0, rows // 8, step, 0)
    for u in range(UNROLL):
        forth[live + u] = rows << 12
        back[live + u] = (rows << 12) | (out.shape[0] * PACKET)
    end = ((live + UNROLL - 1) // UNROLL) * UNROLL
    forth[LIST - 1] = end
    back[LIST - 1] = end
    send_partials(stage, index, meta, total_sum(resid * resid), flag, out)


def next_backward(codes, labels, weight, mine, other, scal, index, held, out, resid_out, scal_out, grow, stage, meta):
    rows = weight.shape[0]
    clear(stage)
    both = mine[rows:, :] + other[rows:, :]
    alpha = jnp.sqrt(gathered_sum(both[0:3, :]) + EPS)
    unit = rhs_of(labels, weight) / scal[0:1, 0:1]
    resid = weight[...] * ((mine[0:rows, :] + other[0:rows, :]) / alpha) - alpha * unit
    resid_out[...] = resid
    scal_out[...] = pair_tile(alpha, both[3:4, 0:1])
    set_rows(grow, weight[...] * resid)
    backward_list(codes, held, grow, stage)
    send_partials(stage, index, meta, total_sum(resid * resid), 0.0, out)


def pair_tile(a, b):
    row = lax.broadcasted_iota(jnp.int32, (8, 128), 0)
    return jnp.where(row == 0, jnp.broadcast_to(a, (8, 128)), jnp.broadcast_to(b, (8, 128)))


def reduced(own, recv):
    lane = lax.broadcasted_iota(jnp.int32, (1, 128), 1) // PACKET
    feature = (lax.broadcasted_iota(jnp.int32, (own, 128), 0) + 1).astype(F32)
    acc = jnp.zeros((own, 128), F32)
    sums = jnp.zeros((1, 128), F32)
    most = jnp.zeros((1, 128), F32)
    for g in range(recv.shape[0] // 4):
        known = jnp.zeros((1, 128), F32)
        for j in range(4):
            row = recv[4 * g + j, PACKET - 8 : PACKET, :].astype(F32)[7:8, :]
            known = known + jnp.where(lane == j, row, 0.0)
            sums = sums + jnp.where(lane == j, 0.0, row)
        most = jnp.maximum(most, known)
        chosen = jnp.where(feature == known, 1.0, 0.0).astype(BF16)
        acc = acc + jnp.dot(chosen, recv[4 * g : 4 * g + 4].reshape(128, 128), preferred_element_type=F32)
    first = lax.broadcasted_iota(jnp.int32, (1, 128), 1) % PACKET == 0
    total = jnp.sum(jnp.where(first, sums, 0.0), axis=1, keepdims=True)
    return acc, jnp.sqrt(total + EPS), jnp.max(most, axis=1, keepdims=True)


def send_step(own, out, step_vec, scale):
    data = (scale * step_vec).astype(BF16)
    tile = spread(total_sum(step_vec * step_vec))

    def put(d, carry):
        out[d, 0:own, :] = data
        out[d, own : own + META, :] = tile
        return carry

    lax.fori_loop(0, out.shape[0], put, 0, unroll=8)


def first_owner(own, recv, scale_hbm, out, step_out, beta_out, scale, sem):
    start = pl.multiple_of(lax.axis_index("rows") * own, own)
    copy = pltpu.make_async_copy(scale_hbm.at[pl.ds(start, own), :], scale, sem)
    copy.start()
    total, beta, most = reduced(own, recv)
    copy.wait()
    step_vec = scale[...] * total / beta
    step_out[...] = step_vec
    beta_out[...] = pair_tile(beta, jnp.where(most > own, 1.0, 0.0))
    send_step(own, out, step_vec, scale[...])


def next_owner(own, recv, step_in, alpha_in, scale_hbm, out, beta_out, scale, sem):
    start = pl.multiple_of(lax.axis_index("rows") * own, own)
    copy = pltpu.make_async_copy(scale_hbm.at[pl.ds(start, own), :], scale, sem)
    copy.start()
    total, beta, _ = reduced(own, recv)
    copy.wait()
    unit = step_in[...] / alpha_in[0:1, 0:1]
    step_vec = scale[...] * total / beta - beta * unit
    beta_out[...] = jnp.broadcast_to(beta, beta_out.shape)
    send_step(own, out, step_vec, scale[...])


def forward(own, codes, recv, scal, held, out, table, *outs):
    rows = out.shape[0] - META
    tiles = own // 8

    def fill(d, meta):
        table[pl.ds(d * tiles, tiles)] = recv[d, 0:own, :].astype(F32).reshape(tiles, 8, 128)
        return meta + recv[d, own : own + META, :].astype(F32)

    meta = lax.fori_loop(0, recv.shape[0], fill, jnp.zeros((META, 128), F32), unroll=8)
    row = lax.broadcasted_iota(jnp.int32, (META, 128), 0)
    out[rows:, :] = jnp.where(row == 3, scal[1:2, :], meta)
    for ref in outs:
        ref[...] = jnp.zeros_like(ref)
    forward_list(codes, held, table, outs)
    acc = outs[0][0 : rows // 8]
    for ref in outs[1:]:
        acc = acc + ref[0 : rows // 8]
    out[0:rows, :] = acc.reshape(rows, 128)


def last_rows(weight, mine, other, resid_in, beta_in, resid_out, alpha_out, out):
    rows = weight.shape[0]
    both = mine[rows:, :] + other[rows:, :]
    alpha = jnp.sqrt(gathered_sum(both[0:3, :]) + EPS)
    unit = resid_in[...] / beta_in[0:1, 0:1]
    resid = weight[...] * ((mine[0:rows, :] + other[0:rows, :]) / alpha) - alpha * unit
    resid_out[...] = resid
    alpha_out[...] = jnp.broadcast_to(alpha, alpha_out.shape)
    out[...] = jnp.broadcast_to(total_sum(resid * resid), out.shape)


def combine(own, recv0, recv1, scale, squares, beta0, alpha0, beta1, alpha1, out_hbm, flag, out, sems):
    b0, a0 = beta0[0:1, 0:1], alpha0[0:1, 0:1]
    b1, a1 = beta1[0:1, 0:1], alpha1[0:1, 0:1]
    b2 = jnp.sqrt(jnp.sum(squares[...], axis=0, keepdims=True)[:, 0:1] + EPS)
    rho1 = jnp.sqrt(a0 * a0 + b1 * b1)
    cos1, sin1 = a0 / rho1, b1 / rho1
    theta1, bar1 = sin1 * a1, -cos1 * a1
    phi1, phibar1 = cos1 * b0, sin1 * b0
    rho2 = jnp.sqrt(bar1 * bar1 + b2 * b2)
    phi2 = (bar1 / rho2) * phibar1
    second = phi2 / rho2
    first = phi1 / rho1 - second * (theta1 / rho1)
    first, second = first / a0, second / a1
    flag[0, 0] = jnp.max(alpha0[1:2, :])
    n = sems.shape[0]
    each = out.shape[0] // n

    def copy(i):
        at = pl.ds(pl.multiple_of(i * each, each), each)
        return pltpu.make_async_copy(out.at[at], out_hbm.at[at], sems.at[i])

    def put(i, carry):
        for j in range(each // own):
            d = i * (each // own) + j
            at = pl.ds(pl.multiple_of(d * own, own), own)
            mixed = first * recv0[d, 0:own, :].astype(F32) + second * recv1[d, 0:own, :].astype(F32)
            out[at, :] = mixed / scale[at, :]
        copy(i).start()
        return carry

    lax.fori_loop(0, n, put, 0)
    lax.fori_loop(0, n, lambda i, carry: (copy(i).wait(), carry)[1], 0)


def general(blocks, col_index, row_counts, labels, row_weight, feature_scale):
    feat_local, side = feature_scale.shape
    peers = lax.axis_size("rows")
    local_col = col_index.T - lax.axis_index("feat") * feat_local
    live = (lax.broadcasted_iota(jnp.int32, local_col.shape, 0) < row_counts.T).astype(F32)

    def over_rows(x):
        return jnp.sum(lax.all_to_all(jnp.broadcast_to(x, (peers, 8, 128)), "rows", 0, 0), axis=0)[0, 0]

    def over_feat(x):
        return x + lax.ppermute(x, "feat", [(0, 1), (1, 0)])

    def backward(resid):
        rowed = (row_weight * resid).astype(BF16)
        terms = jnp.einsum("rsij,ri->srj", blocks, rowed, preferred_element_type=F32) * live[:, :, None]
        partial = jax.ops.segment_sum(terms.reshape(-1, side), local_col.reshape(-1), num_segments=feat_local)
        owned = jnp.sum(lax.all_to_all(partial.reshape(peers, -1, side), "rows", 0, 0), axis=0)
        total = lax.all_to_all(jnp.broadcast_to(owned, (peers,) + owned.shape), "rows", 0, 0).reshape(feat_local, side)
        return total, jnp.sqrt(over_rows(jnp.sum(resid * resid)) + EPS)

    def norm(step_vec):
        return jnp.sqrt(over_feat(jnp.full((8, 128), jnp.sum(step_vec * step_vec)))[0, 0] + EPS)

    resid = row_weight * (2 * labels - 1).astype(F32)
    total, beta = backward(resid)
    step_vec = feature_scale * total / beta
    alpha = norm(step_vec)
    unit_feat = step_vec / alpha
    start = (resid, beta, alpha, unit_feat, beta, alpha, unit_feat, jnp.zeros_like(unit_feat))

    def iteration(_, state):
        resid, beta, alpha, unit_feat, phi_bar, rho_bar, search, result = state
        scaled = (feature_scale * unit_feat).astype(BF16)
        picked = jnp.take(scaled, local_col, axis=0)
        terms = jnp.einsum("rsij,srj->sri", blocks, picked, preferred_element_type=F32)
        resid = row_weight * over_feat(jnp.sum(terms * live[:, :, None], axis=0)) - alpha * (resid / beta)
        total, beta = backward(resid)
        step_vec = feature_scale * total / beta - beta * unit_feat
        alpha = norm(step_vec)
        unit_feat = step_vec / alpha
        rho = jnp.sqrt(rho_bar * rho_bar + beta * beta)
        cosine, sine = rho_bar / rho, beta / rho
        theta, rho_bar = sine * alpha, -cosine * alpha
        phi, phi_bar = cosine * phi_bar, sine * phi_bar
        result = result + phi / rho * search
        search = unit_feat - theta / rho * search
        return (resid, beta, alpha, unit_feat, phi_bar, rho_bar, search, result)

    state = lax.fori_loop(0, ITERS, iteration, start)
    return state[-1], state[0]


def body(blocks, col_index, row_counts, labels, row_weight, feature_scale):
    rows, slots, side, _ = blocks.shape
    feat_local = feature_scale.shape[0]
    peers = lax.axis_size("rows")
    own = feat_local // peers
    far = [pltpu.with_memory_space_constraint(x, pltpu.HBM) for x in (col_index.T, row_counts.T, labels, row_weight)]
    far_blocks = pltpu.with_memory_space_constraint(blocks.reshape(rows * slots, side, side), pltpu.HBM)
    smem = pl.BlockSpec(memory_space=pltpu.SMEM)
    vmem = pl.BlockSpec(memory_space=pltpu.VMEM)
    hbm = pl.BlockSpec(memory_space=pltpu.HBM)
    small = jax.ShapeDtypeStruct((8, 128), F32)
    rowvec = jax.ShapeDtypeStruct((rows, side), F32)
    packet = jax.ShapeDtypeStruct((peers, own + META, side), BF16)
    sparse = jax.ShapeDtypeStruct((peers, PACKET, side), BF16)
    part = jax.ShapeDtypeStruct((rows + META, side), F32)
    listed = jax.ShapeDtypeStruct((LIST,), jnp.int32)
    marked = jax.ShapeDtypeStruct((peers // 8, 8, side), F32)
    params = pltpu.CompilerParams(vmem_limit_bytes=20 << 20)
    table = pltpu.VMEM((feat_local // 8, 8, side), F32)
    stage = pltpu.VMEM((peers * PACKET // 8 + 1, 8, side), F32)
    mark = pltpu.VMEM(marked.shape, F32)
    row_table = pltpu.VMEM((rows // 8 + 1, 8, side), F32)
    scale_scratch = [pltpu.VMEM((own, side), F32), pltpu.SemaphoreType.DMA]

    def exchange(x):
        return lax.all_to_all(x, "rows", 0, 0)

    def swap(x):
        return lax.ppermute(x, "feat", [(0, 1), (1, 0)])

    def forward_part(recv, scal):
        return pl.pallas_call(
            functools.partial(forward, own),
            out_shape=part,
            in_specs=[smem, vmem, vmem, vmem],
            out_specs=vmem,
            scratch_shapes=[table] + [row_table] * TABLES,
            compiler_params=params,
            name="forward",
        )(forth, recv, scal, held)

    send, held, forth, back, index = pl.pallas_call(
        functools.partial(first_backward, own),
        out_shape=(
            sparse,
            pltpu.VMEM((rows * slots, side, side), BF16),
            listed,
            listed,
            marked,
        ),
        in_specs=[hbm] * 5,
        out_specs=(vmem, vmem, smem, smem, vmem),
        scratch_shapes=[
            pltpu.VMEM((slots, rows), jnp.int32),
            pltpu.VMEM((1, rows), jnp.int32),
            pltpu.SMEM((3 * slots, rows), jnp.int32),
            pltpu.VMEM((rows, side), jnp.int32),
            pltpu.VMEM((rows, side), F32),
            pltpu.VMEM((rows, 2 * side), F32),
            pltpu.VMEM((3 * slots, rows), jnp.int32),
            stage,
            mark,
            pltpu.SemaphoreType.DMA((COPIES,)),
            pltpu.SemaphoreType.DMA((5,)),
        ],
        compiler_params=params,
        name="backward0",
    )(*far, far_blocks)
    send, step0, beta0 = pl.pallas_call(
        functools.partial(first_owner, own),
        out_shape=(packet, jax.ShapeDtypeStruct((own, side), F32), small),
        in_specs=[vmem, hbm],
        out_specs=(vmem, vmem, vmem),
        scratch_shapes=scale_scratch,
        compiler_params=params,
        name="owner0",
    )(exchange(send), feature_scale)
    recv0 = exchange(send)
    mine = forward_part(recv0, beta0)
    send, resid1, alpha0 = pl.pallas_call(
        next_backward,
        out_shape=(sparse, rowvec, small),
        in_specs=[smem] + [vmem] * 7,
        out_specs=(vmem, vmem, vmem),
        scratch_shapes=[row_table, stage, mark],
        compiler_params=params,
        name="backward1",
    )(back, labels, row_weight, mine, swap(mine), beta0, index, held)
    send, beta1 = pl.pallas_call(
        functools.partial(next_owner, own),
        out_shape=(packet, small),
        in_specs=[vmem, vmem, vmem, hbm],
        out_specs=(vmem, vmem),
        scratch_shapes=scale_scratch,
        compiler_params=params,
        name="owner1",
    )(exchange(send), step0, alpha0, feature_scale)
    recv1 = exchange(send)
    mine = forward_part(recv1, beta0)
    resid2, alpha1, send = pl.pallas_call(
        last_rows,
        out_shape=(rowvec, small, jax.ShapeDtypeStruct((peers, side), F32)),
        in_specs=[vmem] * 5,
        out_specs=(vmem, vmem, vmem),
        compiler_params=params,
        name="last_rows",
    )(row_weight, mine, swap(mine), resid1, beta1)
    result, flag = pl.pallas_call(
        functools.partial(combine, own),
        out_shape=(jax.ShapeDtypeStruct((feat_local, side), F32), jax.ShapeDtypeStruct((1, 1), F32)),
        in_specs=[vmem] * 8,
        out_specs=(hbm, smem),
        scratch_shapes=[pltpu.VMEM((feat_local, side), F32), pltpu.SemaphoreType.DMA((4,))],
        compiler_params=params,
        name="combine",
    )(recv0, recv1, feature_scale, exchange(send), beta0, alpha0, beta1, alpha1)

    def fits(state):
        return state[0] > 0.0

    def again(state):
        args = (blocks, col_index, row_counts, labels, row_weight, feature_scale)
        return (jnp.zeros_like(state[0]),) + general(*lax.optimization_barrier((state[0],) + args)[1:])

    _, result, resid2 = lax.while_loop(fits, again, (flag.reshape(()), result, resid2))
    return (result, resid2)


def solution(mesh):
    return jax.shard_map(
        body,
        mesh=mesh,
        in_specs=(
            P("rows", "feat", None, None),
            P("rows", "feat"),
            P("rows", "feat"),
            P("rows", None),
            P("rows", None),
            P("feat", None),
        ),
        out_specs=(P("feat", None), P("rows", None)),
        check_vma=False,
    )
```
